512 devices in a mesh: seq: 128 (over y, z, core), ch: 4 (over x).
Axes of the slice: x: 4, y: 4, z: 16, core: 2. Of those that a mesh axis runs over, the one named last changes fastest.
Arguments:
- qkv: bfloat16 [3, 16384, 2048], P(None, 'seq', 'ch'), may hold values from -6 to 6
- filt: float32 [16384, 2048], P('seq', 'ch'), may hold values from -0.1875 to 0.1875
- skip_gain: float32 [2048], P('ch'), may hold values from -4 to 4
- short_weight: float32 [3, 3, 2048], P(None, None, 'ch'), may hold values from -3.5 to 3.5
- w_out: bfloat16 [2048, 2048], P(None, 'ch'), may hold values from -0.125 to 0.125
- g_out: bfloat16 [16384, 2048], P('seq', 'ch'), may hold values from -6 to 6
Outputs:
- output: bfloat16 [16384, 2048], P('seq', 'ch')
- grad_qkv: bfloat16 [3, 16384, 2048], P(None, 'seq', 'ch')
- grad_filter: float32 [16384, 2048], P('seq', 'ch')
The draws below stay inside these ranges and needn't reach their ends.
All inputs are finite; a program needn't handle non-finite values.
Results may differ from the reference program's by a relative error of at most 0.0049.
Values may be sent and summed in bfloat16 or wider, within the bound.
A program may use at most 64 MiB of HBM per device.

```python
import math
import jax
import jax.numpy as jnp
from jax import lax

C = 2048
TOKENS = 16384


def block_levels(own_key, extent, split, low, high):
    loudness = 1.0
    for dim, shards_of in split:
        heights = jax.random.uniform(jax.random.fold_in(jax.random.fold_in(own_key, 6), dim), (shards_of,), jnp.float32, low / len(split), high / len(split))
        loudness = loudness * jnp.repeat(jnp.exp(heights), extent[dim] // shards_of).reshape((-1,) + (1,) * (len(extent) - 1 - dim))
    return loudness


def bell_draw(rng, shape, width, reach, cuts=(), held_as=jnp.bfloat16):
    result = width * jax.random.normal(rng, shape, jnp.float32)
    if cuts:
        result = result * block_levels(rng, shape, cuts, -0.22, 0.18)
    return jnp.clip(result, -reach, reach).astype(held_as)


def setup_inputs(seed: int = 0) -> dict:
    key_list = jax.random.split(jax.random.key(seed), 7)
    return {
        "qkv": bell_draw(key_list[0], (3, TOKENS, C), 1.0, 6.0, ((1, 128), (2, 4))),
        "filt": bell_draw(key_list[1], (TOKENS, C), (TOKENS // 16) ** -0.5, 0.1875, ((0, 128), (1, 4)), jnp.float32),
        "skip_gain": bell_draw(key_list[2], (C,), 1.0, 4.0, ((0, 4),), jnp.float32),
        "short_weight": bell_draw(key_list[3], (3, 3, C), 3 ** -0.5, 3.5, ((2, 4),), jnp.float32),
        "w_out": bell_draw(key_list[4], (C, C), C ** -0.5, 0.125, ((1, 4),)),
        "g_out": bell_draw(key_list[5], (TOKENS, C), 1.0, 6.0, ((0, 128), (1, 4))),
    }


def reference(qkv, filt, skip_gain, short_weight, w_out, g_out):
    token_count = qkv.shape[1]
    padded = jnp.pad(qkv, ((0, 0), (2, 0), (0, 0)))
    short = short_weight[:, 0, None, :] * padded[:, 2:, :] + short_weight[:, 1, None, :] * padded[:, 1:-1, :] + short_weight[:, 2, None, :] * padded[:, :-2, :]
    query_gate = short[0]
    key_short = short[1]
    value_short = short[2]
    mixed = key_short * value_short
    length = 2 * token_count
    mixed_spec = jnp.fft.rfft(mixed, n=length, axis=0)
    kernel_spec = jnp.fft.rfft(filt, n=length, axis=0)
    conv_out = jnp.fft.irfft(mixed_spec * kernel_spec, n=length, axis=0)[:token_count]
    long_out = conv_out + skip_gain * mixed
    gated = (query_gate * long_out).astype(jnp.bfloat16)
    output = jnp.dot(gated, w_out, preferred_element_type=jnp.float32).astype(jnp.bfloat16)
    grad_gated = lax.dot_general(g_out, w_out, (((1,), (1,)), ((), ())), preferred_element_type=jnp.float32)
    grad_long = grad_gated * query_gate
    grad_query = grad_gated * long_out
    grad_spec = jnp.fft.rfft(grad_long, n=length, axis=0)
    correlated = jnp.fft.irfft(jnp.conj(kernel_spec) * grad_spec, n=length, axis=0)[:token_count]
    grad_mixed = correlated + skip_gain * grad_long
    grad_filter = jnp.fft.irfft(jnp.conj(mixed_spec) * grad_spec, n=length, axis=0)[:token_count] * (1.0 / math.sqrt(token_count))
    grad_short = jnp.stack([grad_query, grad_mixed * value_short, grad_mixed * key_short])
    padded_grad = jnp.pad(grad_short, ((0, 0), (0, 2), (0, 0)))
    grad_qkv = (short_weight[:, 0, None, :] * padded_grad[:, :-2, :] + short_weight[:, 1, None, :] * padded_grad[:, 1:-1, :] + short_weight[:, 2, None, :] * padded_grad[:, 2:, :]).astype(jnp.bfloat16)
    return (output, grad_qkv, grad_filter)
```

```python
import math

import jax
import jax.numpy as jnp
import numpy as np
from jax import lax
from jax.sharding import PartitionSpec as P

HIGH = lax.Precision.HIGH
BF16 = jnp.bfloat16
F32 = jnp.float32


def dft_tables(blocks, rows):
    p = np.arange(blocks)[None, :]
    c = np.arange(blocks)[:, None] + 0.5
    outer = 2 * np.pi * p * c / (2 * blocks)
    r = np.arange(rows)[None, :]
    turn = 2 * np.pi * r * c / (2 * blocks * rows)
    inner = 2 * np.pi * np.arange(rows)[:, None] * r / rows
    return [
        np.asarray(f(a), np.float32) for a in (outer, turn, inner) for f in (np.cos, np.sin)
    ]


def local(qkv, filt, skip_gain, short_weight, w_out, g_out):
    blocks = lax.axis_size("seq")
    slabs = lax.axis_size("ch")
    rows, width = qkv.shape[1:]
    own = width // blocks
    oc, os_, tc, ts, ic, is_ = dft_tables(blocks, rows)

    def passed(x, step):
        route = [(i - step, i) for i in range(blocks) if 0 <= i - step < blocks]
        return lax.ppermute(x, "seq", route)

    partial = lax.dot_general(g_out, w_out, (((1,), (1,)), ((), ())), preferred_element_type=F32)
    partial = partial.astype(BF16).reshape(rows, slabs, width)
    parts = lax.all_to_all(partial, "ch", split_axis=1, concat_axis=1, tiled=True)
    grad_gated = jnp.sum(parts.astype(F32), axis=1)

    ext = jnp.concatenate([passed(qkv[:, rows - 2 :, :], 1), qkv], axis=1).astype(F32)
    sw = short_weight[:, :, None, :]
    short = sw[:, 0] * ext[:, 2:] + sw[:, 1] * ext[:, 1:-1] + sw[:, 2] * ext[:, :-2]
    query, key, value = short[0], short[1], short[2]
    mixed = key * value
    grad_long = grad_gated * query

    def spread(signals):
        n = len(signals)
        x = jnp.stack(signals).astype(BF16).transpose(2, 0, 1).reshape(blocks, own * n, rows)
        return lax.all_to_all(x, "seq", split_axis=0, concat_axis=0, tiled=True)

    def gathered(y, n):
        x = lax.all_to_all(y, "seq", split_axis=0, concat_axis=0, tiled=True)
        return x.reshape(width, n, rows).transpose(1, 2, 0).astype(F32)

    def mm(pattern, a, b):
        return jnp.einsum(pattern, a, b, precision=HIGH, preferred_element_type=F32)

    x = spread([mixed, filt, grad_long]).astype(F32)
    outer = np.concatenate([oc, -os_], axis=0)
    s = mm("ap,pnr->nar", outer, x)
    sre, sim = s[:, :blocks], s[:, blocks:]
    tre = sre * tc + sim * ts
    tim = sim * tc - sre * ts
    w = np.block([[ic, -is_], [is_, ic]])
    spec = mm("ncr,rk->nck", jnp.concatenate([tre, tim], axis=2), w)
    spec = spec.reshape(own, 3, blocks, 2, rows)
    mre, mim = spec[:, 0, :, 0], spec[:, 0, :, 1]
    fre, fim = spec[:, 1, :, 0], spec[:, 1, :, 1]
    gre, gim = spec[:, 2, :, 0], spec[:, 2, :, 1]
    pre = jnp.stack([mre * fre - mim * fim, fre * gre + fim * gim, mre * gre + mim * gim], 1)
    pim = jnp.stack([mre * fim + mim * fre, fre * gim - fim * gre, mre * gim - mim * gre], 1)
    wi = np.block([[ic, is_], [-is_, ic]])
    z = mm("nsck,kr->nscr", jnp.concatenate([pre, pim], axis=3), wi)
    zre, zim = z[..., :rows], z[..., rows:]
    yre = zre * tc - zim * ts
    yim = zim * tc + zre * ts
    y = jnp.concatenate([yre, yim], axis=2).reshape(own * 3, 2 * blocks, rows)
    back = np.concatenate([oc.T, -os_.T], axis=1) * np.float32(1.0 / (blocks * rows))
    t = mm("pa,nar->pnr", back, y).astype(BF16)
    conv, corr, gfil = gathered(t, 3)

    long_out = conv + skip_gain * mixed
    gated = (query * long_out).astype(BF16)
    sent = jnp.broadcast_to(gated[:, None], (rows, slabs, width))
    every = lax.all_to_all(sent, "ch", split_axis=1, concat_axis=1, tiled=True)
    output = jnp.dot(
        every.reshape(rows, slabs * width), w_out, preferred_element_type=F32
    ).astype(BF16)
    grad_query = grad_gated * long_out
    grad_mixed = corr + skip_gain * grad_long
    grad_filter = gfil * (1.0 / math.sqrt(blocks * rows))
    gs = jnp.stack([grad_query, grad_mixed * value, grad_mixed * key])
    extg = jnp.concatenate([gs, passed(gs[:, :2, :], -1)], axis=1)
    grad_qkv = sw[:, 0] * extg[:, :-2] + sw[:, 1] * extg[:, 1:-1] + sw[:, 2] * extg[:, 2:]
    return (output, grad_qkv.astype(BF16), grad_filter)


def solution(mesh):
    in_specs = (
        P(None, "seq", "ch"),
        P("seq", "ch"),
        P("ch"),
        P(None, None, "ch"),
        P(None, "ch"),
        P("seq", "ch"),
    )
    out_specs = (P("seq", "ch"), P(None, "seq", "ch"), P("seq", "ch"))
    return jax.shard_map(local, mesh=mesh, in_specs=in_specs, out_specs=out_specs, check_vma=False)
```

```python
import functools
import math

import jax
import jax.numpy as jnp
import numpy as np
from jax import lax
from jax.experimental import pallas as pl
from jax.experimental.pallas import tpu as pltpu
from jax.sharding import PartitionSpec as P

BF16 = jnp.bfloat16
F32 = jnp.float32
MESH = pl.DeviceIdType.MESH
Z_CHIPS = 16
OWN = 4
FILT, MIXED, GRAD, CONV, CORR, GFIL = range(6)


def split_const(a):
    high = a.astype(BF16)
    return high, (a - high.astype(np.float64)).astype(BF16)


def dft_tables(blocks, rows, z_chips):
    q = np.arange(blocks)
    yc, z = q // z_chips, q % z_chips
    p = ((yc // 2) * z_chips + z) * 2 + yc % 2
    c = np.arange(blocks)[:, None] + 0.5
    outer = 2 * np.pi * p[None, :] * c / (2 * blocks)
    r = np.arange(rows)[None, :]
    turn = 2 * np.pi * r * c / (2 * blocks * rows)
    inner = 2 * np.pi * np.arange(rows)[:, None] * r / rows
    ahead = np.concatenate([np.cos(outer), -np.sin(outer)], axis=0)
    ic, is_ = np.cos(inner), np.sin(inner)
    mix = np.block([[ic, -is_], [is_, ic]])
    unmix = np.block([[ic, is_], [-is_, ic]])
    return (
        *split_const(ahead),
        *split_const(ahead.T / (blocks * rows)),
        *split_const(mix),
        *split_const(unmix),
        np.cos(turn).astype(np.float32),
        np.sin(turn).astype(np.float32),
    )


def dot(a, b):
    return jnp.dot(a, b, preferred_element_type=F32)


def halves(a):
    high = a.astype(BF16)
    return high, (a - high.astype(F32)).astype(BF16)


def kernel(
    shape,
    qkv, filt, skip, sw, w_out, g_out,
    ah, al, bh, bl, mh, ml, uh, ul, tcos, tsin,
    output, grad_qkv, grad_filter,
    send, mid, recv, halo, ghalo_out, ghalo_in, part_out, part_in, gate_out, gate_in,
    xs, ext, spec, gs, shorts, gg, glong,
    send1, recv1, send2, recv2, loc1, loc2, hsem, psend, precv, gsend, grecv,
):
    blocks, zn, slabs, rows, width = shape
    lines = blocks // zn
    s = lax.axis_index("seq")
    ch = lax.axis_index("ch")
    core = s % 2
    z = (s // 2) % zn
    y = s // (2 * zn)
    yc = y * 2 + core

    def on_z(i):
        dz = zn // 2 + ((i + 1) // 2) * (1 - 2 * (i % 2))
        other = (z + dz) % zn
        return other, (y * zn + other) * 2 + core

    def on_line(i):
        other = (yc + 1 + i) % lines
        return other, ((other // 2) * zn + z) * 2 + other % 2

    after = (s + 1) % blocks
    before = (s + blocks - 1) % blocks

    barrier = pltpu.get_barrier_semaphore()

    def greet(a, b):
        pl.semaphore_signal(barrier, inc=1, device_id=(a, b), device_id_type=MESH)

    def greet_z(i, _):
        greet(on_z(i)[1], ch)
        return 0

    def greet_line(i, _):
        greet(on_line(i)[1], ch)
        return 0

    lax.fori_loop(0, zn - 1, greet_z, 0)
    lax.fori_loop(0, lines - 1, greet_line, 0)
    for i in range(1, slabs):
        greet(s, (ch + i) % slabs)
    greet(after, ch)
    greet(before, ch)

    def slab(k):
        return w_out[pl.ds(pl.multiple_of(k * width, width), width), :]

    def rows_of(k):
        return lax.dot_general(
            g_out[...], slab(k), (((1,), (1,)), ((), ())), preferred_element_type=F32
        )

    def pack(u, value):
        send[u] = jnp.swapaxes(value, 0, 1).astype(BF16).reshape(lines, zn, OWN, rows)

    def unpack(u):
        return jnp.swapaxes(recv[u].astype(F32).reshape(width, rows), 0, 1)

    def own1(u):
        return pltpu.make_async_copy(send.at[u, :, z], mid.at[u, z], loc1.at[u])

    def own2(u):
        return pltpu.make_async_copy(mid.at[u, :, yc], recv.at[u, yc], loc2.at[u])

    def start1(u):
        def go(i, _):
            other, device = on_z(i)
            pltpu.make_async_remote_copy(
                src_ref=send.at[u, :, other],
                dst_ref=mid.at[u, z],
                send_sem=send1.at[u],
                recv_sem=recv1.at[u],
                device_id=(device, ch),
                device_id_type=MESH,
            ).start()
            return 0

        lax.fori_loop(0, zn - 1, go, 0)
        own1(u).start()

    def start2(u):
        own1(u).wait()
        landed = mid.at[u, pl.ds(0, zn - 1)]
        pltpu.make_async_copy(landed, landed, recv1.at[u]).wait()

        def go(i, _):
            other, device = on_line(i)
            pltpu.make_async_remote_copy(
                src_ref=mid.at[u, :, other],
                dst_ref=recv.at[u, yc],
                send_sem=send2.at[u],
                recv_sem=recv2.at[u],
                device_id=(device, ch),
                device_id_type=MESH,
            ).start()
            return 0

        lax.fori_loop(0, lines - 1, go, 0)
        own2(u).start()

    def finish(u):
        own2(u).wait()
        landed = recv.at[u, pl.ds(0, lines - 1)]
        pltpu.make_async_copy(landed, landed, recv2.at[u]).wait()

    def drain(u):
        sent = mid.at[u, pl.ds(0, zn - 1)]
        pltpu.make_async_copy(sent, sent, send1.at[u]).wait()
        sent = recv.at[u, pl.ds(0, lines - 1)]
        pltpu.make_async_copy(sent, sent, send2.at[u]).wait()

    def to_slab(i, k, src, dst, ssem, rsem):
        return pltpu.make_async_remote_copy(
            src_ref=src,
            dst_ref=dst,
            send_sem=ssem.at[i],
            recv_sem=rsem.at[i],
            device_id=(s, k),
            device_id_type=MESH,
        )

    halo_copy = pltpu.make_async_remote_copy(
        src_ref=qkv.at[:, pl.ds(rows - 8, 8), :],
        dst_ref=halo,
        send_sem=hsem.at[0],
        recv_sem=hsem.at[1],
        device_id=(after, ch),
        device_id_type=MESH,
    )
    ghalo_copy = pltpu.make_async_remote_copy(
        src_ref=ghalo_out,
        dst_ref=ghalo_in,
        send_sem=hsem.at[2],
        recv_sem=hsem.at[3],
        device_id=(before, ch),
        device_id_type=MESH,
    )
    part_copies = [
        to_slab(i, (ch + i + 1) % slabs, part_out.at[i], part_in.at[i], psend, precv)
        for i in range(slabs - 1)
    ]
    gate_copies = [
        to_slab(i, (ch + i + 1) % slabs, gate_out, gate_in.at[i], gsend, grecv)
        for i in range(slabs - 1)
    ]

    def ahead(u, k):
        xs[...] = recv[u].astype(F32).reshape(width, rows)
        x = jnp.concatenate(
            [xs[pl.ds(j, blocks, stride=OWN), :] for j in range(OWN)], axis=1
        ).astype(BF16)
        t = dot(ah[...], x) + dot(al[...], x)
        tc, ts = tcos[...], tsin[...]
        turned = []
        for j in range(OWN):
            re = t[:blocks, j * rows : (j + 1) * rows]
            im = t[blocks:, j * rows : (j + 1) * rows]
            turned.append(jnp.concatenate([re * tc + im * ts, im * tc - re * ts], axis=1))
        high, low = halves(jnp.concatenate(turned, axis=0))
        spec[k] = dot(high, mh[...]) + dot(low, mh[...]) + dot(high, ml[...])

    def back(u, re, im):
        high, low = halves(jnp.concatenate([re, im], axis=1))
        t = dot(high, uh[...]) + dot(low, uh[...]) + dot(high, ul[...])
        tc, ts = tcos[...], tsin[...]
        turned = []
        for j in range(OWN):
            re = t[j * blocks : (j + 1) * blocks, :rows]
            im = t[j * blocks : (j + 1) * blocks, rows:]
            turned.append(jnp.concatenate([re * tc - im * ts, im * tc + re * ts], axis=0))
        high, low = halves(jnp.concatenate(turned, axis=1))
        t = dot(bh[...], high) + dot(bl[...], high) + dot(bh[...], low)
        for j in range(OWN):
            xs[pl.ds(j, blocks, stride=OWN), :] = t[:, j * rows : (j + 1) * rows]
        send[u] = xs[...].astype(BF16).reshape(lines, zn, OWN, rows)

    for i in range(slabs - 1):
        part_out[i] = rows_of((ch + i + 1) % slabs).astype(BF16)
    pack(FILT, filt[...])
    gg[...] = rows_of(ch)
    pl.semaphore_wait(barrier, zn - 1 + lines - 1 + slabs - 1 + 2)

    halo_copy.start()
    for copy in part_copies:
        copy.start()
    start1(FILT)

    halo_copy.wait_recv()
    for i in range(3):
        head = halo[i].astype(F32)
        ext[pl.ds(0, 8), :] = jnp.where(s > 0, head, jnp.zeros_like(head))
        ext[pl.ds(8, rows), :] = qkv[i].astype(F32)
        shorts[i] = (
            sw[i, pl.ds(0, 1), :] * ext[pl.ds(8, rows), :]
            + sw[i, pl.ds(1, 1), :] * ext[pl.ds(7, rows), :]
            + sw[i, pl.ds(2, 1), :] * ext[pl.ds(6, rows), :]
        )
    pack(MIXED, shorts[1] * shorts[2])
    start1(MIXED)

    total = gg[...]
    for i in range(slabs - 1):
        part_copies[i].wait_recv()
        total = total + part_in[i].astype(F32)
    gg[...] = total
    glong[...] = total * shorts[0]
    pack(GRAD, glong[...])
    start1(GRAD)

    start2(FILT)
    start2(MIXED)
    finish(FILT)
    ahead(FILT, 0)
    finish(MIXED)
    ahead(MIXED, 1)

    fre, fim = spec[0, :, :rows], spec[0, :, rows:]
    mre, mim = spec[1, :, :rows], spec[1, :, rows:]
    back(CONV, mre * fre - mim * fim, mre * fim + mim * fre)
    start1(CONV)
    start2(GRAD)
    finish(GRAD)
    ahead(GRAD, 2)
    fre, fim = spec[0, :, :rows], spec[0, :, rows:]
    gre, gim = spec[2, :, :rows], spec[2, :, rows:]
    back(CORR, fre * gre + fim * gim, fre * gim - fim * gre)
    start1(CORR)
    start2(CONV)
    mre, mim = spec[1, :, :rows], spec[1, :, rows:]
    gre, gim = spec[2, :, :rows], spec[2, :, rows:]
    back(GFIL, mre * gre + mim * gim, mre * gim - mim * gre)
    start1(GFIL)

    finish(CONV)
    long_out = unpack(CONV) + skip[...] * (shorts[1] * shorts[2])
    gate_out[...] = (shorts[0] * long_out).astype(BF16)
    for copy in gate_copies:
        copy.start()
    gs[0] = gg[...] * long_out

    start2(CORR)
    total = dot(gate_out[...], slab(ch))
    for i in range(slabs - 1):
        gate_copies[i].wait_recv()
        total = total + dot(gate_in[i], slab((ch + slabs - 1 - i) % slabs))
    output[...] = total.astype(BF16)

    start2(GFIL)
    finish(CORR)
    grad_mixed = unpack(CORR) + skip[...] * glong[...]
    gs[1] = grad_mixed * shorts[2]
    gs[2] = grad_mixed * shorts[1]
    ghalo_out[...] = gs[:, pl.ds(0, 8), :]
    ghalo_copy.start()

    finish(GFIL)
    grad_filter[...] = unpack(GFIL) * (1.0 / math.sqrt(blocks * rows))

    ghalo_copy.wait_recv()
    for i in range(3):
        tail = ghalo_in[i]
        ext[pl.ds(0, rows), :] = gs[i]
        ext[pl.ds(rows, 8), :] = jnp.where(s < blocks - 1, tail, jnp.zeros_like(tail))
        grad_qkv[i] = (
            sw[i, pl.ds(0, 1), :] * ext[pl.ds(0, rows), :]
            + sw[i, pl.ds(1, 1), :] * ext[pl.ds(1, rows), :]
            + sw[i, pl.ds(2, 1), :] * ext[pl.ds(2, rows), :]
        ).astype(BF16)

    halo_copy.wait_send()
    ghalo_copy.wait_send()
    for copy in part_copies + gate_copies:
        copy.wait_send()
    for u in range(6):
        drain(u)


def local(qkv, filt, skip_gain, short_weight, w_out, g_out):
    blocks = lax.axis_size("seq")
    slabs = lax.axis_size("ch")
    rows, width = qkv.shape[1:]
    zn = Z_CHIPS
    lines = blocks // zn
    tables = dft_tables(blocks, rows, zn)
    vmem = pl.BlockSpec(memory_space=pltpu.VMEM)
    unit = (6, lines, zn, OWN, rows)
    dma = pltpu.SemaphoreType.DMA
    return pl.pallas_call(
        functools.partial(kernel, (blocks, zn, slabs, rows, width)),
        out_shape=(
            jax.ShapeDtypeStruct((rows, width), BF16),
            jax.ShapeDtypeStruct((3, rows, width), BF16),
            jax.ShapeDtypeStruct((rows, width), F32),
        ),
        in_specs=[vmem] * (6 + len(tables)),
        out_specs=(vmem, vmem, vmem),
        scratch_shapes=[
            pltpu.VMEM(unit, BF16),
            pltpu.VMEM((6, zn, lines, OWN, rows), BF16),
            pltpu.VMEM(unit, BF16),
            pltpu.VMEM((3, 8, width), BF16),
            pltpu.VMEM((3, 8, width), F32),
            pltpu.VMEM((3, 8, width), F32),
            pltpu.VMEM((slabs - 1, rows, width), BF16),
            pltpu.VMEM((slabs - 1, rows, width), BF16),
            pltpu.VMEM((rows, width), BF16),
            pltpu.VMEM((slabs - 1, rows, width), BF16),
            pltpu.VMEM((width, rows), F32),
            pltpu.VMEM((rows + 8, width), F32),
            pltpu.VMEM((3, OWN * blocks, 2 * rows), F32),
            pltpu.VMEM((3, rows, width), F32),
            pltpu.VMEM((3, rows, width), F32),
            pltpu.VMEM((rows, width), F32),
            pltpu.VMEM((rows, width), F32),
            dma((6,)), dma((6,)), dma((6,)), dma((6,)), dma((6,)), dma((6,)),
            dma((4,)),
            dma((slabs - 1,)), dma((slabs - 1,)), dma((slabs - 1,)), dma((slabs - 1,)),
        ],
        compiler_params=pltpu.CompilerParams(collective_id=0, has_side_effects=True),
    )(qkv, filt, skip_gain[None, :], short_weight, w_out, g_out, *tables)


def solution(mesh):
    in_specs = (
        P(None, "seq", "ch"),
        P("seq", "ch"),
        P("ch"),
        P(None, None, "ch"),
        P(None, "ch"),
        P("seq", "ch"),
    )
    out_specs = (P("seq", "ch"), P(None, "seq", "ch"), P("seq", "ch"))
    return jax.shard_map(local, mesh=mesh, in_specs=in_specs, out_specs=out_specs, check_vma=False)
```

```python
import functools
import math

import jax
import jax.numpy as jnp
import numpy as np
from jax import lax
from jax.experimental import pallas as pl
from jax.experimental.pallas import tpu as pltpu
from jax.sharding import PartitionSpec as P

BF16 = jnp.bfloat16
F32 = jnp.float32
MESH = pl.DeviceIdType.MESH
Z_CHIPS = 16
VMEM_LIMIT = 67043328
HALVES = 2
OWN = 2
FILT, MIXED, GRAD, CONV, CORR, GFIL = (HALVES * i for i in range(6))
UNITS = 6 * HALVES


def split_const(a):
    high = a.astype(BF16)
    return high, (a - high.astype(np.float64)).astype(BF16)


def dft_tables(blocks, rows, z_chips):
    q = np.arange(blocks)
    lines = blocks // z_chips
    z, yc = q // lines, q % lines
    p = ((yc // 2) * z_chips + z) * 2 + yc % 2
    c = np.arange(blocks)[:, None] + 0.5
    outer = 2 * np.pi * p[None, :] * c / (2 * blocks)
    r = np.arange(rows)[None, :]
    turn = 2 * np.pi * r * c / (2 * blocks * rows)
    inner = 2 * np.pi * np.arange(rows)[:, None] * r / rows
    ahead = np.concatenate([np.cos(outer), -np.sin(outer)], axis=0)
    ic, is_ = np.cos(inner), np.sin(inner)
    mix = np.block([[ic, -is_], [is_, ic]])
    unmix = np.block([[ic, is_], [-is_, ic]])
    return (
        *split_const(ahead),
        *split_const(ahead.T / (blocks * rows)),
        *split_const(mix),
        *split_const(unmix),
        np.cos(turn).astype(np.float32),
        np.sin(turn).astype(np.float32),
    )


def dot(a, b):
    return jnp.dot(a, b, preferred_element_type=F32)


def halves(a):
    high = a.astype(BF16)
    return high, (a - high.astype(F32)).astype(BF16)


def kernel(shape, *refs):
    inputs, results = refs[:16], refs[16:19]
    kept, loaded = refs[19:35], refs[35]
    body(shape, inputs, kept, loaded, *results, *refs[36:])


def body(
    shape, inputs, kept, loaded,
    output, grad_qkv, grad_filter,
    send, mid, recv, halo, ghalo_out, ghalo_in, part_out, part_in, gate_out, gate_in,
    xs, ext, spec, gs, shorts, gg, glong,
    send1, recv1, send2, recv2, loc1, loc2, hsem, psend, precv, gsend, grecv,
):
    blocks, zn, slabs, rows, width = shape
    qkv, filt, skip, sw, w_out, g_out, ah, al, bh, bl, mh, ml, uh, ul, tcos, tsin = kept
    lines = blocks // zn
    s = lax.axis_index("seq")
    ch = lax.axis_index("ch")
    core = s % 2
    z = (s // 2) % zn
    y = s // (2 * zn)
    yc = y * 2 + core

    def on_z(i):
        dz = zn // 2 + ((i + 1) // 2) * (1 - 2 * (i % 2))
        other = (z + dz) % zn
        return other, (y * zn + other) * 2 + core

    def on_line(i):
        other = (yc + 1 + i) % lines
        return other, ((other // 2) * zn + z) * 2 + other % 2

    after = (s + 1) % blocks
    before = (s + blocks - 1) % blocks

    barrier = pltpu.get_barrier_semaphore()

    def greet(a, b):
        pl.semaphore_signal(barrier, inc=1, device_id=(a, b), device_id_type=MESH)

    def greet_z(i, _):
        greet(on_z(i)[1], ch)
        return 0

    def greet_line(i, _):
        greet(on_line(i)[1], ch)
        return 0

    lax.fori_loop(0, zn - 1, greet_z, 0)
    lax.fori_loop(0, lines - 1, greet_line, 0)
    for i in range(1, slabs):
        greet(s, (ch + i) % slabs)
    greet(after, ch)
    greet(before, ch)

    loads = [
        pltpu.make_async_copy(src, dst, loaded.at[i])
        for i, (src, dst) in enumerate(zip(inputs, kept))
    ]
    for i in (5, 4, 1, 0, 3, 2):
        loads[i].start()
    for copy in loads[6:]:
        copy.start()

    def slab(k):
        return w_out[pl.ds(pl.multiple_of(k * width, width), width), :]

    def rows_of(k):
        return lax.dot_general(
            g_out[...], slab(k), (((1,), (1,)), ((), ())), preferred_element_type=F32
        )

    group = width // HALVES

    def columns(h):
        return pl.ds(h * group, group)

    def pack(u, value):
        send[u] = jnp.swapaxes(value, 0, 1).astype(BF16).reshape(zn, lines, OWN, rows)

    def unpack(u):
        return jnp.swapaxes(recv[u].astype(F32).reshape(group, rows), 0, 1)

    def own1(u):
        return pltpu.make_async_copy(send.at[u, z], mid.at[u, z], loc1.at[u])

    def own2(u):
        return pltpu.make_async_copy(mid.at[u, :, yc], recv.at[u, :, yc], loc2.at[u])

    def start1(u):
        def go(i, _):
            other, device = on_z(i)
            pltpu.make_async_remote_copy(
                src_ref=send.at[u, other],
                dst_ref=mid.at[u, z],
                send_sem=send1.at[u],
                recv_sem=recv1.at[u],
                device_id=(device, ch),
                device_id_type=MESH,
            ).start()
            return 0

        lax.fori_loop(0, zn - 1, go, 0)
        own1(u).start()

    def start2(u):
        own1(u).wait()
        landed = mid.at[u, pl.ds(0, zn - 1)]
        pltpu.make_async_copy(landed, landed, recv1.at[u]).wait()

        def go(i, _):
            other, device = on_line(i)
            pltpu.make_async_remote_copy(
                src_ref=mid.at[u, :, other],
                dst_ref=recv.at[u, :, yc],
                send_sem=send2.at[u],
                recv_sem=recv2.at[u],
                device_id=(device, ch),
                device_id_type=MESH,
            ).start()
            return 0

        lax.fori_loop(0, lines - 1, go, 0)
        own2(u).start()

    def finish(u):
        own2(u).wait()
        landed = recv.at[u, :, pl.ds(0, lines - 1)]
        pltpu.make_async_copy(landed, landed, recv2.at[u]).wait()

    def drain(u):
        sent = mid.at[u, pl.ds(0, zn - 1)]
        pltpu.make_async_copy(sent, sent, send1.at[u]).wait()
        sent = recv.at[u, :, pl.ds(0, lines - 1)]
        pltpu.make_async_copy(sent, sent, send2.at[u]).wait()

    def to_slab(i, k, src, dst, ssem, rsem):
        return pltpu.make_async_remote_copy(
            src_ref=src,
            dst_ref=dst,
            send_sem=ssem.at[i],
            recv_sem=rsem.at[i],
            device_id=(s, k),
            device_id_type=MESH,
        )

    halo_copy = pltpu.make_async_remote_copy(
        src_ref=qkv.at[:, pl.ds(rows - 8, 8), :],
        dst_ref=halo,
        send_sem=hsem.at[0],
        recv_sem=hsem.at[1],
        device_id=(after, ch),
        device_id_type=MESH,
    )
    ghalo_copy = pltpu.make_async_remote_copy(
        src_ref=ghalo_out,
        dst_ref=ghalo_in,
        send_sem=hsem.at[2],
        recv_sem=hsem.at[3],
        device_id=(before, ch),
        device_id_type=MESH,
    )
    part_copies = [
        to_slab(i, (ch + i + 1) % slabs, part_out.at[i], part_in.at[i], psend, precv)
        for i in range(slabs - 1)
    ]
    gate_copies = [
        to_slab(i, (ch + i + 1) % slabs, gate_out, gate_in.at[i], gsend, grecv)
        for i in range(slabs - 1)
    ]

    def ahead(u, k):
        xs[...] = recv[u].astype(F32).reshape(group, rows)
        x = jnp.concatenate(
            [xs[pl.ds(j, blocks, stride=OWN), :] for j in range(OWN)], axis=1
        ).astype(BF16)
        t = dot(ah[...], x) + dot(al[...], x)
        tc, ts = tcos[...], tsin[...]
        turned = []
        for j in range(OWN):
            re = t[:blocks, j * rows : (j + 1) * rows]
            im = t[blocks:, j * rows : (j + 1) * rows]
            turned.append(jnp.concatenate([re * tc + im * ts, im * tc - re * ts], axis=1))
        high, low = halves(jnp.concatenate(turned, axis=0))
        spec[k] = dot(high, mh[...]) + dot(low, mh[...]) + dot(high, ml[...])

    def back(u, re, im):
        high, low = halves(jnp.concatenate([re, im], axis=1))
        t = dot(high, uh[...]) + dot(low, uh[...]) + dot(high, ul[...])
        tc, ts = tcos[...], tsin[...]
        turned = []
        for j in range(OWN):
            re = t[j * blocks : (j + 1) * blocks, :rows]
            im = t[j * blocks : (j + 1) * blocks, rows:]
            turned.append(jnp.concatenate([re * tc - im * ts, im * tc + re * ts], axis=0))
        high, low = halves(jnp.concatenate(turned, axis=1))
        t = dot(bh[...], high) + dot(bl[...], high) + dot(bh[...], low)
        for j in range(OWN):
            xs[pl.ds(j, blocks, stride=OWN), :] = t[:, j * rows : (j + 1) * rows]
        send[u] = xs[...].astype(BF16).reshape(zn, lines, OWN, rows)

    def spectra(k, h):
        k = k + h
        return spec[k, :, :rows], spec[k, :, rows:]

    def convolve(h):
        (mre, mim), (fre, fim) = spectra(MIXED, h), spectra(FILT, h)
        back(CONV + h, mre * fre - mim * fim, mre * fim + mim * fre)
        start1(CONV + h)

    def correlate(u, k, h):
        (are, aim), (gre, gim) = spectra(k, h), spectra(GRAD, h)
        back(u + h, are * gre + aim * gim, are * gim - aim * gre)
        start1(u + h)

    def land(u):
        finish(u)
        ahead(u, u)

    loads[5].wait()
    loads[4].wait()
    for i in range(slabs - 1):
        part_out[i] = rows_of((ch + i + 1) % slabs).astype(BF16)
    loads[1].wait()
    for h in range(HALVES):
        pack(FILT + h, filt[:, columns(h)])
    gg[...] = rows_of(ch)
    for i in (0, 3, 2):
        loads[i].wait()
    pl.semaphore_wait(barrier, zn - 1 + lines - 1 + slabs - 1 + 2)

    halo_copy.start()
    start1(FILT)
    for copy in part_copies:
        copy.start()

    halo_copy.wait_recv()
    for i in (1, 2, 0):
        head = halo[i].astype(F32)
        ext[pl.ds(0, 8), :] = jnp.where(s > 0, head, jnp.zeros_like(head))
        ext[pl.ds(8, rows), :] = qkv[i].astype(F32)
        shorts[i] = (
            sw[i, pl.ds(0, 1), :] * ext[pl.ds(8, rows), :]
            + sw[i, pl.ds(1, 1), :] * ext[pl.ds(7, rows), :]
            + sw[i, pl.ds(2, 1), :] * ext[pl.ds(6, rows), :]
        )
        if i == 2:
            for h in range(HALVES):
                pack(MIXED + h, shorts[1, :, columns(h)] * shorts[2, :, columns(h)])
                start1(MIXED + h)
                if h + 1 < HALVES:
                    start1(FILT + h + 1)

    total = gg[...]
    for i in range(slabs - 1):
        part_copies[i].wait_recv()
        total = total + part_in[i].astype(F32)
    gg[...] = total
    glong[...] = total * shorts[0]
    for h in range(HALVES):
        pack(GRAD + h, glong[:, columns(h)])
        start1(GRAD + h)

    start2(FILT)
    start2(MIXED)
    for copy in loads[6:]:
        copy.wait()
    land(FILT)
    start2(FILT + 1)
    land(MIXED)
    convolve(0)
    start2(MIXED + 1)
    land(FILT + 1)
    start2(GRAD)
    land(MIXED + 1)
    convolve(1)
    start2(GRAD + 1)
    land(GRAD)
    correlate(CORR, FILT, 0)
    correlate(GFIL, MIXED, 0)
    start2(CONV)
    land(GRAD + 1)
    correlate(CORR, FILT, 1)
    correlate(GFIL, MIXED, 1)
    start2(CONV + 1)
    start2(CORR)

    for h in range(HALVES):
        finish(CONV + h)
        at = columns(h)
        mixed = shorts[1, :, at] * shorts[2, :, at]
        long_out = unpack(CONV + h) + skip[:, at] * mixed
        gate_out[:, at] = (shorts[0, :, at] * long_out).astype(BF16)
        gs[0, :, at] = gg[:, at] * long_out
    for copy in gate_copies:
        copy.start()
    total = dot(gate_out[...], slab(ch))

    start2(GFIL)

    def mix_grads(h):
        finish(CORR + h)
        at = columns(h)
        grad_mixed = unpack(CORR + h) + skip[:, at] * glong[:, at]
        gs[1, :, at] = grad_mixed * shorts[2, :, at]
        gs[2, :, at] = grad_mixed * shorts[1, :, at]

    def filter_grads(h):
        finish(GFIL + h)
        grad_filter[:, columns(h)] = unpack(GFIL + h) * (1.0 / math.sqrt(blocks * rows))

    mix_grads(0)
    start2(CORR + 1)
    filter_grads(0)
    start2(GFIL + 1)
    mix_grads(1)
    ghalo_out[...] = gs[:, pl.ds(0, 8), :]
    ghalo_copy.start()

    for i in range(slabs - 1):
        gate_copies[i].wait_recv()
        total = total + dot(gate_in[i], slab((ch + slabs - 1 - i) % slabs))
    output[...] = total.astype(BF16)

    ghalo_copy.wait_recv()
    for i in range(3):
        tail = ghalo_in[i]
        ext[pl.ds(0, rows), :] = gs[i]
        ext[pl.ds(rows, 8), :] = jnp.where(s < blocks - 1, tail, jnp.zeros_like(tail))
        grad_qkv[i] = (
            sw[i, pl.ds(0, 1), :] * ext[pl.ds(0, rows), :]
            + sw[i, pl.ds(1, 1), :] * ext[pl.ds(1, rows), :]
            + sw[i, pl.ds(2, 1), :] * ext[pl.ds(2, rows), :]
        ).astype(BF16)
    filter_grads(1)

    halo_copy.wait_send()
    ghalo_copy.wait_send()
    for copy in part_copies + gate_copies:
        copy.wait_send()
    for u in range(UNITS):
        drain(u)


def write_out(*refs):
    ins, outs, held, sem = refs[:3], refs[3:6], refs[6:9], refs[9]
    pulls = [pltpu.make_async_copy(ins[i], held[i], sem.at[i]) for i in range(3)]
    pushes = [pltpu.make_async_copy(held[i], outs[i], sem.at[i + 3]) for i in range(3)]
    for copy in pulls:
        copy.start()
    for pull, push in zip(pulls, pushes):
        pull.wait()
        push.start()
    for copy in pushes:
        copy.wait()


def local(qkv, filt, skip_gain, short_weight, w_out, g_out):
    blocks = lax.axis_size("seq")
    slabs = lax.axis_size("ch")
    rows, width = qkv.shape[1:]
    zn = Z_CHIPS
    lines = blocks // zn
    tables = dft_tables(blocks, rows, zn)
    args = (qkv, filt, skip_gain[None, :], short_weight, w_out, g_out, *tables)
    vmem = pl.BlockSpec(memory_space=pltpu.VMEM)
    unit = (UNITS, zn, lines, OWN, rows)
    dma = pltpu.SemaphoreType.DMA
    results = pl.pallas_call(
        functools.partial(kernel, (blocks, zn, slabs, rows, width)),
        out_shape=(
            jax.ShapeDtypeStruct((rows, width), BF16),
            jax.ShapeDtypeStruct((3, rows, width), BF16),
            jax.ShapeDtypeStruct((rows, width), F32),
        ),
        in_specs=[pl.BlockSpec(memory_space=pltpu.HBM)] * len(args),
        out_specs=(vmem, vmem, vmem),
        scratch_shapes=[
            *[pltpu.VMEM(a.shape, a.dtype) for a in args],
            dma((len(args),)),
            pltpu.VMEM(unit, BF16),
            pltpu.VMEM(unit, BF16),
            pltpu.VMEM(unit, BF16),
            pltpu.VMEM((3, 8, width), BF16),
            pltpu.VMEM((3, 8, width), F32),
            pltpu.VMEM((3, 8, width), F32),
            pltpu.VMEM((slabs - 1, rows, width), BF16),
            pltpu.VMEM((slabs - 1, rows, width), BF16),
            pltpu.VMEM((rows, width), BF16),
            pltpu.VMEM((slabs - 1, rows, width), BF16),
            pltpu.VMEM((OWN * blocks, rows), F32),
            pltpu.VMEM((rows + 8, width), F32),
            pltpu.VMEM((3 * HALVES, OWN * blocks, 2 * rows), F32),
            pltpu.VMEM((3, rows, width), F32),
            pltpu.VMEM((3, rows, width), F32),
            pltpu.VMEM((rows, width), F32),
            pltpu.VMEM((rows, width), F32),
            *[dma((UNITS,))] * 6,
            dma((4,)),
            dma((slabs - 1,)), dma((slabs - 1,)), dma((slabs - 1,)), dma((slabs - 1,)),
        ],
        compiler_params=pltpu.CompilerParams(
            collective_id=0, has_side_effects=True, vmem_limit_bytes=VMEM_LIMIT
        ),
    )(*args)
    return pl.pallas_call(
        write_out,
        out_shape=tuple(jax.ShapeDtypeStruct(r.shape, r.dtype) for r in results),
        in_specs=[pl.BlockSpec(memory_space=pltpu.HBM)] * 3,
        out_specs=[pl.BlockSpec(memory_space=pltpu.HBM)] * 3,
        scratch_shapes=[*[pltpu.VMEM(r.shape, r.dtype) for r in results], dma((6,))],
        compiler_params=pltpu.CompilerParams(vmem_limit_bytes=VMEM_LIMIT),
    )(*results)


def solution(mesh):
    in_specs = (
        P(None, "seq", "ch"),
        P("seq", "ch"),
        P("ch"),
        P(None, None, "ch"),
        P(None, "ch"),
        P("seq", "ch"),
    )
    out_specs = (P("seq", "ch"), P(None, "seq", "ch"), P("seq", "ch"))
    return jax.shard_map(local, mesh=mesh, in_specs=in_specs, out_specs=out_specs, check_vma=False)
```

```python
import functools
import math

import jax
import jax.numpy as jnp
import numpy as np
from jax import lax
from jax.experimental import pallas as pl
from jax.experimental.pallas import tpu as pltpu
from jax.sharding import PartitionSpec as P

BF16 = jnp.bfloat16
F32 = jnp.float32
MESH = pl.DeviceIdType.MESH
Z_CHIPS = 16
VMEM_LIMIT = 67043328
HALVES = 2
OWN = 2
FILT, MIXED, GRAD, CONV, CORR, GFIL = (HALVES * i for i in range(6))
UNITS = 6 * HALVES
LINE_FIRST = (FILT + 1, MIXED + 1, GRAD, GRAD + 1, CORR + 1, GFIL, GFIL + 1)


def split_const(a):
    high = a.astype(BF16)
    return high, (a - high.astype(np.float64)).astype(BF16)


def dft_tables(blocks, rows, z_chips):
    q = np.arange(blocks)
    lines = blocks // z_chips
    z, yc = q // lines, q % lines
    p = ((yc // 2) * z_chips + z) * 2 + yc % 2
    c = np.arange(blocks)[:, None] + 0.5
    outer = 2 * np.pi * p[None, :] * c / (2 * blocks)
    r = np.arange(rows)[None, :]
    turn = 2 * np.pi * r * c / (2 * blocks * rows)
    inner = 2 * np.pi * np.arange(rows)[:, None] * r / rows
    ahead = np.concatenate([np.cos(outer), -np.sin(outer)], axis=0)
    ic, is_ = np.cos(inner), np.sin(inner)
    mix = np.block([[ic, -is_], [is_, ic]])
    unmix = np.block([[ic, is_], [-is_, ic]])
    return (
        *split_const(ahead),
        *split_const(ahead.T / (blocks * rows)),
        *split_const(mix),
        *split_const(unmix),
        np.cos(turn).astype(np.float32),
        np.sin(turn).astype(np.float32),
    )


def dot(a, b):
    return jnp.dot(a, b, preferred_element_type=F32)


def halves(a):
    high = a.astype(BF16)
    return high, (a - high.astype(F32)).astype(BF16)


def kernel(shape, *refs):
    inputs, results = refs[:16], refs[16:19]
    kept, loaded = refs[19:35], refs[35]
    body(shape, inputs, kept, loaded, *results, *refs[36:])


def body(
    shape, inputs, kept, loaded,
    output, grad_qkv, grad_filter,
    send, mid, recv, halo, ghalo_out, ghalo_in, part_out, part_in, gate_out, gate_in,
    xs, ext, spec, gs, shorts, gg, glong,
    send1, recv1, send2, recv2, loc1, loc2, hsem, psend, precv, gsend, grecv,
):
    blocks, zn, slabs, rows, width = shape
    qkv, filt, skip, sw, w_out, g_out, ah, al, bh, bl, mh, ml, uh, ul, tcos, tsin = kept
    lines = blocks // zn
    s = lax.axis_index("seq")
    ch = lax.axis_index("ch")
    core = s % 2
    z = (s // 2) % zn
    y = s // (2 * zn)
    yc = y * 2 + core

    def on_z(i):
        dz = zn // 2 + ((i + 1) // 2) * (1 - 2 * (i % 2))
        other = (z + dz) % zn
        return other, (y * zn + other) * 2 + core

    def on_line(i):
        other = (yc + 1 + i) % lines
        return other, ((other // 2) * zn + z) * 2 + other % 2

    after = (s + 1) % blocks
    before = (s + blocks - 1) % blocks

    barrier = pltpu.get_barrier_semaphore()

    def greet(a, b):
        pl.semaphore_signal(barrier, inc=1, device_id=(a, b), device_id_type=MESH)

    def greet_z(i, _):
        greet(on_z(i)[1], ch)
        return 0

    def greet_line(i, _):
        greet(on_line(i)[1], ch)
        return 0

    lax.fori_loop(0, zn - 1, greet_z, 0)
    lax.fori_loop(0, lines - 1, greet_line, 0)
    for i in range(1, slabs):
        greet(s, (ch + i) % slabs)
    greet(after, ch)
    greet(before, ch)

    loads = [
        pltpu.make_async_copy(src, dst, loaded.at[i])
        for i, (src, dst) in enumerate(zip(inputs, kept))
    ]
    for i in (5, 4, 1, 0, 3, 2):
        loads[i].start()
    for copy in loads[6:]:
        copy.start()

    def slab(k):
        return w_out[pl.ds(pl.multiple_of(k * width, width), width), :]

    def rows_of(k):
        return lax.dot_general(
            g_out[...], slab(k), (((1,), (1,)), ((), ())), preferred_element_type=F32
        )

    group = width // HALVES

    def columns(h):
        return pl.ds(h * group, group)

    def pack(u, value):
        send[u] = jnp.swapaxes(value, 0, 1).astype(BF16).reshape(zn, lines, OWN, rows)

    def unpack(u):
        return jnp.swapaxes(recv[u].astype(F32).reshape(group, rows), 0, 1)

    def on_lines(u, src, dst, ssem, rsem, lsem):
        def go(i, _):
            other, device = on_line(i)
            pltpu.make_async_remote_copy(
                src_ref=src.at[u, :, other],
                dst_ref=dst.at[u, :, yc],
                send_sem=ssem.at[u],
                recv_sem=rsem.at[u],
                device_id=(device, ch),
                device_id_type=MESH,
            ).start()
            return 0

        lax.fori_loop(0, lines - 1, go, 0)
        pltpu.make_async_copy(src.at[u, :, yc], dst.at[u, :, yc], lsem.at[u]).start()

    def on_zs(u, src, dst, ssem, rsem, lsem):
        def go(i, _):
            other, device = on_z(i)
            pltpu.make_async_remote_copy(
                src_ref=src.at[u, other],
                dst_ref=dst.at[u, z],
                send_sem=ssem.at[u],
                recv_sem=rsem.at[u],
                device_id=(device, ch),
                device_id_type=MESH,
            ).start()
            return 0

        lax.fori_loop(0, zn - 1, go, 0)
        pltpu.make_async_copy(src.at[u, z], dst.at[u, z], lsem.at[u]).start()

    def moved(u, buf, by_line, sem):
        part = buf.at[u, :, pl.ds(0, lines - 1)] if by_line else buf.at[u, pl.ds(0, zn - 1)]
        pltpu.make_async_copy(part, part, sem.at[u]).wait()

    def arrived(u, buf, by_line, rsem, lsem):
        own = buf.at[u, :, yc] if by_line else buf.at[u, z]
        pltpu.make_async_copy(own, own, lsem.at[u]).wait()
        moved(u, buf, by_line, rsem)

    def first(u):
        go = on_lines if u in LINE_FIRST else on_zs
        go(u, send, mid, send1, recv1, loc1)

    def second(u):
        arrived(u, mid, u in LINE_FIRST, recv1, loc1)
        go = on_zs if u in LINE_FIRST else on_lines
        go(u, mid, recv, send2, recv2, loc2)

    def finish(u):
        arrived(u, recv, u not in LINE_FIRST, recv2, loc2)

    def drain(u):
        moved(u, mid, u in LINE_FIRST, send1)
        moved(u, recv, u not in LINE_FIRST, send2)

    def to_slab(i, k, src, dst, ssem, rsem):
        return pltpu.make_async_remote_copy(
            src_ref=src,
            dst_ref=dst,
            send_sem=ssem.at[*i],
            recv_sem=rsem.at[*i],
            device_id=(s, k),
            device_id_type=MESH,
        )

    halo_copy = pltpu.make_async_remote_copy(
        src_ref=qkv.at[:, pl.ds(rows - 8, 8), :],
        dst_ref=halo,
        send_sem=hsem.at[0],
        recv_sem=hsem.at[1],
        device_id=(after, ch),
        device_id_type=MESH,
    )
    ghalo_copy = pltpu.make_async_remote_copy(
        src_ref=ghalo_out,
        dst_ref=ghalo_in,
        send_sem=hsem.at[2],
        recv_sem=hsem.at[3],
        device_id=(before, ch),
        device_id_type=MESH,
    )
    others = range(slabs - 1)
    part_copies = [
        [
            to_slab((h, i), (ch + i + 1) % slabs, part_out.at[h, i], part_in.at[h, i], psend, precv)
            for i in others
        ]
        for h in range(HALVES)
    ]
    gate_copies = [
        [
            to_slab((h, i), (ch + i + 1) % slabs, gate_out.at[h], gate_in.at[h, i], gsend, grecv)
            for i in others
        ]
        for h in range(HALVES)
    ]

    def ahead(u, k):
        xs[...] = recv[u].astype(F32).reshape(group, rows)
        x = jnp.concatenate(
            [xs[pl.ds(j, blocks, stride=OWN), :] for j in range(OWN)], axis=1
        ).astype(BF16)
        t = dot(ah[...], x) + dot(al[...], x)
        tc, ts = tcos[...], tsin[...]
        turned = []
        for j in range(OWN):
            re = t[:blocks, j * rows : (j + 1) * rows]
            im = t[blocks:, j * rows : (j + 1) * rows]
            turned.append(jnp.concatenate([re * tc + im * ts, im * tc - re * ts], axis=1))
        high, low = halves(jnp.concatenate(turned, axis=0))
        spec[k] = dot(high, mh[...]) + dot(low, mh[...]) + dot(high, ml[...])

    def back(u, re, im):
        high, low = halves(jnp.concatenate([re, im], axis=1))
        t = dot(high, uh[...]) + dot(low, uh[...]) + dot(high, ul[...])
        tc, ts = tcos[...], tsin[...]
        turned = []
        for j in range(OWN):
            re = t[j * blocks : (j + 1) * blocks, :rows]
            im = t[j * blocks : (j + 1) * blocks, rows:]
            turned.append(jnp.concatenate([re * tc - im * ts, im * tc + re * ts], axis=0))
        high, low = halves(jnp.concatenate(turned, axis=1))
        t = dot(bh[...], high) + dot(bl[...], high) + dot(bh[...], low)
        for j in range(OWN):
            xs[pl.ds(j, blocks, stride=OWN), :] = t[:, j * rows : (j + 1) * rows]
        send[u] = xs[...].astype(BF16).reshape(zn, lines, OWN, rows)

    def spectra(k, h):
        k = k + h
        return spec[k, :, :rows], spec[k, :, rows:]

    def convolve(h):
        (mre, mim), (fre, fim) = spectra(MIXED, h), spectra(FILT, h)
        back(CONV + h, mre * fre - mim * fim, mre * fim + mim * fre)
        first(CONV + h)

    def correlate(u, k, h):
        (are, aim), (gre, gim) = spectra(k, h), spectra(GRAD, h)
        back(u + h, are * gre + aim * gim, are * gim - aim * gre)
        first(u + h)

    def land(u):
        finish(u)
        ahead(u, u)

    loads[5].wait()
    loads[4].wait()
    for i in others:
        part = rows_of((ch + i + 1) % slabs).astype(BF16)
        for h in range(HALVES):
            part_out[h, i] = part[:, h * group : (h + 1) * group]
    loads[1].wait()
    for h in range(HALVES):
        pack(FILT + h, filt[:, columns(h)])
    gg[...] = rows_of(ch)
    for i in (0, 3, 2):
        loads[i].wait()
    pl.semaphore_wait(barrier, zn - 1 + lines - 1 + slabs - 1 + 2)

    halo_copy.start()
    first(FILT)
    first(FILT + 1)
    for copies in part_copies:
        for copy in copies:
            copy.start()

    def shorten(i):
        head = halo[i].astype(F32)
        ext[pl.ds(0, 8), :] = jnp.where(s > 0, head, jnp.zeros_like(head))
        ext[pl.ds(8, rows), :] = qkv[i].astype(F32)
        shorts[i] = (
            sw[i, pl.ds(0, 1), :] * ext[pl.ds(8, rows), :]
            + sw[i, pl.ds(1, 1), :] * ext[pl.ds(7, rows), :]
            + sw[i, pl.ds(2, 1), :] * ext[pl.ds(6, rows), :]
        )

    halo_copy.wait_recv()
    shorten(1)
    shorten(2)
    for h in range(HALVES):
        pack(MIXED + h, shorts[1, :, columns(h)] * shorts[2, :, columns(h)])
        first(MIXED + h)
    second(FILT + 1)
    shorten(0)

    def long_grads(h):
        at = columns(h)
        total = gg[:, at]
        for i in others:
            part_copies[h][i].wait_recv()
            total = total + part_in[h, i].astype(F32)
        gg[:, at] = total
        glong[:, at] = total * shorts[0, :, at]
        pack(GRAD + h, glong[:, at])
        first(GRAD + h)

    long_grads(0)
    second(MIXED + 1)
    long_grads(1)
    second(FILT)
    second(GRAD)
    second(GRAD + 1)
    second(MIXED)
    for copy in loads[6:]:
        copy.wait()
    land(FILT)
    land(FILT + 1)
    land(MIXED)
    convolve(0)
    land(MIXED + 1)
    convolve(1)
    land(GRAD)
    correlate(CORR, FILT, 0)
    correlate(GFIL, MIXED, 0)
    land(GRAD + 1)
    correlate(CORR, FILT, 1)
    second(GFIL)
    correlate(GFIL, MIXED, 1)
    second(CONV)
    second(CORR + 1)
    second(GFIL + 1)
    second(CONV + 1)

    def gate(h):
        finish(CONV + h)
        at = columns(h)
        mixed = shorts[1, :, at] * shorts[2, :, at]
        long_out = unpack(CONV + h) + skip[:, at] * mixed
        gate_out[h] = (shorts[0, :, at] * long_out).astype(BF16)
        for copy in gate_copies[h]:
            copy.start()
        gs[0, :, at] = gg[:, at] * long_out

    def mix_grads(h):
        finish(CORR + h)
        at = columns(h)
        grad_mixed = unpack(CORR + h) + skip[:, at] * glong[:, at]
        gs[1, :, at] = grad_mixed * shorts[2, :, at]
        gs[2, :, at] = grad_mixed * shorts[1, :, at]

    def filter_grads(h):
        finish(GFIL + h)
        grad_filter[:, columns(h)] = unpack(GFIL + h) * (1.0 / math.sqrt(blocks * rows))

    def half_slab(k, h):
        start = pl.multiple_of(k * width + h * group, group)
        return w_out[pl.ds(start, group), :]

    gate(0)
    second(CORR)
    gate(1)
    total = dot(gate_out[0], half_slab(ch, 0))
    for h in range(1, HALVES):
        total = total + dot(gate_out[h], half_slab(ch, h))
    filter_grads(0)
    mix_grads(0)
    mix_grads(1)
    ghalo_out[...] = gs[:, pl.ds(0, 8), :]
    ghalo_copy.start()

    for h in range(HALVES):
        for i in others:
            gate_copies[h][i].wait_recv()
            total = total + dot(gate_in[h, i], half_slab((ch + slabs - 1 - i) % slabs, h))
    output[...] = total.astype(BF16)

    ghalo_copy.wait_recv()
    for i in range(3):
        tail = ghalo_in[i]
        ext[pl.ds(0, rows), :] = gs[i]
        ext[pl.ds(rows, 8), :] = jnp.where(s < blocks - 1, tail, jnp.zeros_like(tail))
        grad_qkv[i] = (
            sw[i, pl.ds(0, 1), :] * ext[pl.ds(0, rows), :]
            + sw[i, pl.ds(1, 1), :] * ext[pl.ds(1, rows), :]
            + sw[i, pl.ds(2, 1), :] * ext[pl.ds(2, rows), :]
        ).astype(BF16)
    filter_grads(1)

    halo_copy.wait_send()
    ghalo_copy.wait_send()
    for copies in part_copies + gate_copies:
        for copy in copies:
            copy.wait_send()
    for u in range(UNITS):
        drain(u)


def write_out(*refs):
    ins, outs, held, sem = refs[:3], refs[3:6], refs[6:9], refs[9]
    pulls = [pltpu.make_async_copy(ins[i], held[i], sem.at[i]) for i in range(3)]
    pushes = [pltpu.make_async_copy(held[i], outs[i], sem.at[i + 3]) for i in range(3)]
    for copy in pulls:
        copy.start()
    for pull, push in zip(pulls, pushes):
        pull.wait()
        push.start()
    for copy in pushes:
        copy.wait()


def local(qkv, filt, skip_gain, short_weight, w_out, g_out):
    blocks = lax.axis_size("seq")
    slabs = lax.axis_size("ch")
    rows, width = qkv.shape[1:]
    zn = Z_CHIPS
    lines = blocks // zn
    tables = dft_tables(blocks, rows, zn)
    args = (qkv, filt, skip_gain[None, :], short_weight, w_out, g_out, *tables)
    vmem = pl.BlockSpec(memory_space=pltpu.VMEM)
    unit = (UNITS, zn, lines, OWN, rows)
    dma = pltpu.SemaphoreType.DMA
    results = pl.pallas_call(
        functools.partial(kernel, (blocks, zn, slabs, rows, width)),
        out_shape=(
            jax.ShapeDtypeStruct((rows, width), BF16),
            jax.ShapeDtypeStruct((3, rows, width), BF16),
            jax.ShapeDtypeStruct((rows, width), F32),
        ),
        in_specs=[pl.BlockSpec(memory_space=pltpu.HBM)] * len(args),
        out_specs=(vmem, vmem, vmem),
        scratch_shapes=[
            *[pltpu.VMEM(a.shape, a.dtype) for a in args],
            dma((len(args),)),
            pltpu.VMEM(unit, BF16),
            pltpu.VMEM(unit, BF16),
            pltpu.VMEM(unit, BF16),
            pltpu.VMEM((3, 8, width), BF16),
            pltpu.VMEM((3, 8, width), F32),
            pltpu.VMEM((3, 8, width), F32),
            pltpu.VMEM((HALVES, slabs - 1, rows, width // HALVES), BF16),
            pltpu.VMEM((HALVES, slabs - 1, rows, width // HALVES), BF16),
            pltpu.VMEM((HALVES, rows, width // HALVES), BF16),
            pltpu.VMEM((HALVES, slabs - 1, rows, width // HALVES), BF16),
            pltpu.VMEM((OWN * blocks, rows), F32),
            pltpu.VMEM((rows + 8, width), F32),
            pltpu.VMEM((3 * HALVES, OWN * blocks, 2 * rows), F32),
            pltpu.VMEM((3, rows, width), F32),
            pltpu.VMEM((3, rows, width), F32),
            pltpu.VMEM((rows, width), F32),
            pltpu.VMEM((rows, width), F32),
            *[dma((UNITS,))] * 6,
            dma((4,)),
            *[dma((HALVES, slabs - 1))] * 4,
        ],
        compiler_params=pltpu.CompilerParams(
            collective_id=0, has_side_effects=True, vmem_limit_bytes=VMEM_LIMIT
        ),
    )(*args)
    return pl.pallas_call(
        write_out,
        out_shape=tuple(jax.ShapeDtypeStruct(r.shape, r.dtype) for r in results),
        in_specs=[pl.BlockSpec(memory_space=pltpu.HBM)] * 3,
        out_specs=[pl.BlockSpec(memory_space=pltpu.HBM)] * 3,
        scratch_shapes=[*[pltpu.VMEM(r.shape, r.dtype) for r in results], dma((6,))],
        compiler_params=pltpu.CompilerParams(vmem_limit_bytes=VMEM_LIMIT),
    )(*results)


def solution(mesh):
    in_specs = (
        P(None, "seq", "ch"),
        P("seq", "ch"),
        P("ch"),
        P(None, None, "ch"),
        P(None, "ch"),
        P("seq", "ch"),
    )
    out_specs = (P("seq", "ch"), P(None, "seq", "ch"), P("seq", "ch"))
    return jax.shard_map(local, mesh=mesh, in_specs=in_specs, out_specs=out_specs, check_vma=False)
```

```python
import functools
import math

import jax
import jax.numpy as jnp
import numpy as np
from jax import lax
from jax.experimental import pallas as pl
from jax.experimental.pallas import tpu as pltpu
from jax.sharding import PartitionSpec as P

BF16 = jnp.bfloat16
F32 = jnp.float32
MESH = pl.DeviceIdType.MESH
Z_CHIPS = 16
VMEM_LIMIT = 32 * 1024 * 1024
HALVES = 2
OWN = 2
FILT, MIXED, GRAD, CONV, CORR, GFIL = (HALVES * i for i in range(6))
UNITS = 6 * HALVES
LINE_FIRST = (FILT + 1, MIXED + 1, GRAD, GRAD + 1, CORR + 1, GFIL, GFIL + 1)


def split_const(a):
    high = a.astype(BF16)
    return high, (a - high.astype(np.float64)).astype(BF16)


def dft_tables(blocks, rows, z_chips):
    q = np.arange(blocks)
    lines = blocks // z_chips
    z, yc = q // lines, q % lines
    p = ((yc // 2) * z_chips + z) * 2 + yc % 2
    c = np.arange(blocks)[:, None] + 0.5
    outer = 2 * np.pi * p[None, :] * c / (2 * blocks)
    r = np.arange(rows)[None, :]
    turn = 2 * np.pi * r * c / (2 * blocks * rows)
    inner = 2 * np.pi * np.arange(rows)[:, None] * r / rows
    ahead = np.concatenate([np.cos(outer), -np.sin(outer)], axis=0)
    ic, is_ = np.cos(inner), np.sin(inner)
    mix = np.block([[ic, -is_], [is_, ic]])
    unmix = np.block([[ic, is_], [-is_, ic]])
    return (
        *split_const(ahead),
        *split_const(ahead.T / (blocks * rows)),
        *split_const(mix),
        *split_const(unmix),
        np.cos(turn).astype(np.float32),
        np.sin(turn).astype(np.float32),
    )


def dot(a, b):
    return jnp.dot(a, b, preferred_element_type=F32)


def halves(a):
    high = a.astype(BF16)
    return high, (a - high.astype(F32)).astype(BF16)


def kernel(shape, *refs):
    inputs, results = refs[:16], refs[16:19]
    kept, loaded = refs[19:35], refs[35]
    body(shape, inputs, kept, loaded, *results, *refs[36:])


def body(
    shape, inputs, kept, loaded,
    output, grad_qkv, grad_filter,
    send, mid, recv, halo, ghalo_out, ghalo_in, part_out, part_in, gate_out, gate_in,
    xs, ext, spec, gs, shorts, gg, glong,
    send1, recv1, send2, recv2, loc1, loc2, hsem, psend, precv, gsend, grecv,
):
    blocks, zn, slabs, rows, width = shape
    qkv, filt, skip, sw, w_out, g_out, ah, al, bh, bl, mh, ml, uh, ul, tcos, tsin = kept
    lines = blocks // zn
    s = lax.axis_index("seq")
    ch = lax.axis_index("ch")
    core = s % 2
    z = (s // 2) % zn
    y = s // (2 * zn)
    yc = y * 2 + core

    def on_z(i):
        dz = zn // 2 + ((i + 1) // 2) * (1 - 2 * (i % 2))
        other = (z + dz) % zn
        return other, (y * zn + other) * 2 + core

    def on_line(i):
        other = (yc + 1 + i) % lines
        return other, ((other // 2) * zn + z) * 2 + other % 2

    after = (s + 1) % blocks
    before = (s + blocks - 1) % blocks

    barrier = pltpu.get_barrier_semaphore()

    def greet(a, b):
        pl.semaphore_signal(barrier, inc=1, device_id=(a, b), device_id_type=MESH)

    def greet_z(i, _):
        greet(on_z(i)[1], ch)
        return 0

    def greet_line(i, _):
        greet(on_line(i)[1], ch)
        return 0

    lax.fori_loop(0, zn - 1, greet_z, 0)
    lax.fori_loop(0, lines - 1, greet_line, 0)
    for i in range(1, slabs):
        greet(s, (ch + i) % slabs)
    greet(after, ch)
    greet(before, ch)

    loads = [
        pltpu.make_async_copy(src, dst, loaded.at[i])
        for i, (src, dst) in enumerate(zip(inputs, kept))
    ]
    for i in (5, 4, 1, 0, 3, 2):
        loads[i].start()
    for copy in loads[6:]:
        copy.start()

    def slab(k):
        return w_out[pl.ds(pl.multiple_of(k * width, width), width), :]

    def rows_of(k):
        return lax.dot_general(
            g_out[...], slab(k), (((1,), (1,)), ((), ())), preferred_element_type=F32
        )

    group = width // HALVES

    def columns(h):
        return pl.ds(h * group, group)

    def pack(u, value):
        send[u] = jnp.swapaxes(value, 0, 1).astype(BF16).reshape(zn, lines, OWN, rows)

    def unpack(u):
        return jnp.swapaxes(recv[u].astype(F32).reshape(group, rows), 0, 1)

    def on_lines(u, src, dst, ssem, rsem, lsem):
        def go(i, _):
            other, device = on_line(i)
            pltpu.make_async_remote_copy(
                src_ref=src.at[u, :, other],
                dst_ref=dst.at[u, :, yc],
                send_sem=ssem.at[u],
                recv_sem=rsem.at[u],
                device_id=(device, ch),
                device_id_type=MESH,
            ).start()
            return 0

        lax.fori_loop(0, lines - 1, go, 0)
        pltpu.make_async_copy(src.at[u, :, yc], dst.at[u, :, yc], lsem.at[u]).start()

    def on_zs(u, src, dst, ssem, rsem, lsem):
        def go(i, _):
            other, device = on_z(i)
            pltpu.make_async_remote_copy(
                src_ref=src.at[u, other],
                dst_ref=dst.at[u, z],
                send_sem=ssem.at[u],
                recv_sem=rsem.at[u],
                device_id=(device, ch),
                device_id_type=MESH,
            ).start()
            return 0

        lax.fori_loop(0, zn - 1, go, 0)
        pltpu.make_async_copy(src.at[u, z], dst.at[u, z], lsem.at[u]).start()

    def moved(u, buf, by_line, sem):
        part = buf.at[u, :, pl.ds(0, lines - 1)] if by_line else buf.at[u, pl.ds(0, zn - 1)]
        pltpu.make_async_copy(part, part, sem.at[u]).wait()

    def arrived(u, buf, by_line, rsem, lsem):
        own = buf.at[u, :, yc] if by_line else buf.at[u, z]
        pltpu.make_async_copy(own, own, lsem.at[u]).wait()
        moved(u, buf, by_line, rsem)

    def first(u):
        go = on_lines if u in LINE_FIRST else on_zs
        go(u, send, mid, send1, recv1, loc1)

    def second(u):
        arrived(u, mid, u in LINE_FIRST, recv1, loc1)
        go = on_zs if u in LINE_FIRST else on_lines
        go(u, mid, recv, send2, recv2, loc2)

    def finish(u):
        arrived(u, recv, u not in LINE_FIRST, recv2, loc2)

    def drain(u):
        moved(u, mid, u in LINE_FIRST, send1)
        moved(u, recv, u not in LINE_FIRST, send2)

    def to_slab(i, k, src, dst, ssem, rsem):
        return pltpu.make_async_remote_copy(
            src_ref=src,
            dst_ref=dst,
            send_sem=ssem.at[*i],
            recv_sem=rsem.at[*i],
            device_id=(s, k),
            device_id_type=MESH,
        )

    halo_copy = pltpu.make_async_remote_copy(
        src_ref=qkv.at[:, pl.ds(rows - 8, 8), :],
        dst_ref=halo,
        send_sem=hsem.at[0],
        recv_sem=hsem.at[1],
        device_id=(after, ch),
        device_id_type=MESH,
    )
    ghalo_copy = pltpu.make_async_remote_copy(
        src_ref=ghalo_out,
        dst_ref=ghalo_in,
        send_sem=hsem.at[2],
        recv_sem=hsem.at[3],
        device_id=(before, ch),
        device_id_type=MESH,
    )
    others = range(slabs - 1)
    part_copies = [
        [
            to_slab((h, i), (ch + i + 1) % slabs, part_out.at[h, i], part_in.at[h, i], psend, precv)
            for i in others
        ]
        for h in range(HALVES)
    ]
    gate_copies = [
        [
            to_slab((h, i), (ch + i + 1) % slabs, gate_out.at[h], gate_in.at[h, i], gsend, grecv)
            for i in others
        ]
        for h in range(HALVES)
    ]

    def ahead(u, k):
        xs[...] = recv[u].astype(F32).reshape(group, rows)
        x = jnp.concatenate(
            [xs[pl.ds(j, blocks, stride=OWN), :] for j in range(OWN)], axis=1
        ).astype(BF16)
        t = dot(ah[...], x) + dot(al[...], x)
        tc, ts = tcos[...], tsin[...]
        turned = []
        for j in range(OWN):
            re = t[:blocks, j * rows : (j + 1) * rows]
            im = t[blocks:, j * rows : (j + 1) * rows]
            turned.append(jnp.concatenate([re * tc + im * ts, im * tc - re * ts], axis=1))
        high, low = halves(jnp.concatenate(turned, axis=0))
        spec[k] = dot(high, mh[...]) + dot(low, mh[...]) + dot(high, ml[...])

    def back(u, re, im):
        high, low = halves(jnp.concatenate([re, im], axis=1))
        t = dot(high, uh[...]) + dot(low, uh[...]) + dot(high, ul[...])
        tc, ts = tcos[...], tsin[...]
        turned = []
        for j in range(OWN):
            re = t[j * blocks : (j + 1) * blocks, :rows]
            im = t[j * blocks : (j + 1) * blocks, rows:]
            turned.append(jnp.concatenate([re * tc - im * ts, im * tc + re * ts], axis=0))
        high, low = halves(jnp.concatenate(turned, axis=1))
        t = dot(bh[...], high) + dot(bl[...], high) + dot(bh[...], low)
        for j in range(OWN):
            xs[pl.ds(j, blocks, stride=OWN), :] = t[:, j * rows : (j + 1) * rows]
        send[u] = xs[...].astype(BF16).reshape(zn, lines, OWN, rows)

    def spectra(k, h):
        k = k + h
        return spec[k, :, :rows], spec[k, :, rows:]

    def convolve(h):
        (mre, mim), (fre, fim) = spectra(MIXED, h), spectra(FILT, h)
        back(CONV + h, mre * fre - mim * fim, mre * fim + mim * fre)
        first(CONV + h)

    def correlate(u, k, h):
        (are, aim), (gre, gim) = spectra(k, h), spectra(GRAD, h)
        back(u + h, are * gre + aim * gim, are * gim - aim * gre)
        first(u + h)

    def land(u):
        finish(u)
        ahead(u, u)

    loads[5].wait()
    loads[4].wait()
    for i in others:
        part = rows_of((ch + i + 1) % slabs).astype(BF16)
        for h in range(HALVES):
            part_out[h, i] = part[:, h * group : (h + 1) * group]
    loads[1].wait()
    for h in range(HALVES):
        pack(FILT + h, filt[:, columns(h)])
    gg[...] = rows_of(ch)
    for i in (0, 3, 2):
        loads[i].wait()
    pl.semaphore_wait(barrier, zn - 1 + lines - 1 + slabs - 1 + 2)

    halo_copy.start()
    first(FILT)
    first(FILT + 1)
    for copies in part_copies:
        for copy in copies:
            copy.start()

    def shorten(i):
        head = halo[i].astype(F32)
        ext[pl.ds(0, 8), :] = jnp.where(s > 0, head, jnp.zeros_like(head))
        ext[pl.ds(8, rows), :] = qkv[i].astype(F32)
        shorts[i] = (
            sw[i, pl.ds(0, 1), :] * ext[pl.ds(8, rows), :]
            + sw[i, pl.ds(1, 1), :] * ext[pl.ds(7, rows), :]
            + sw[i, pl.ds(2, 1), :] * ext[pl.ds(6, rows), :]
        )

    halo_copy.wait_recv()
    shorten(1)
    shorten(2)
    for h in range(HALVES):
        pack(MIXED + h, shorts[1, :, columns(h)] * shorts[2, :, columns(h)])
        first(MIXED + h)
    second(FILT + 1)
    shorten(0)

    def long_grads(h):
        at = columns(h)
        total = gg[:, at]
        for i in others:
            part_copies[h][i].wait_recv()
            total = total + part_in[h, i].astype(F32)
        gg[:, at] = total
        glong[:, at] = total * shorts[0, :, at]
        pack(GRAD + h, glong[:, at])
        first(GRAD + h)

    long_grads(0)
    second(MIXED + 1)
    long_grads(1)
    second(FILT)
    second(GRAD)
    second(GRAD + 1)
    second(MIXED)
    for copy in loads[6:]:
        copy.wait()
    land(FILT)
    land(FILT + 1)
    land(MIXED)
    convolve(0)
    land(MIXED + 1)
    convolve(1)
    land(GRAD)
    correlate(CORR, FILT, 0)
    correlate(GFIL, MIXED, 0)
    land(GRAD + 1)
    correlate(CORR, FILT, 1)
    second(GFIL)
    correlate(GFIL, MIXED, 1)
    second(CONV)
    second(CORR + 1)
    second(GFIL + 1)
    second(CONV + 1)

    def gate(h):
        finish(CONV + h)
        at = columns(h)
        mixed = shorts[1, :, at] * shorts[2, :, at]
        long_out = unpack(CONV + h) + skip[:, at] * mixed
        gate_out[h] = (shorts[0, :, at] * long_out).astype(BF16)
        for copy in gate_copies[h]:
            copy.start()
        gs[0, :, at] = gg[:, at] * long_out

    def mix_grads(h):
        finish(CORR + h)
        at = columns(h)
        grad_mixed = unpack(CORR + h) + skip[:, at] * glong[:, at]
        gs[1, :, at] = grad_mixed * shorts[2, :, at]
        gs[2, :, at] = grad_mixed * shorts[1, :, at]

    def filter_grads(h):
        finish(GFIL + h)
        grad_filter[:, columns(h)] = unpack(GFIL + h) * (1.0 / math.sqrt(blocks * rows))

    def half_slab(k, h):
        start = pl.multiple_of(k * width + h * group, group)
        return w_out[pl.ds(start, group), :]

    gate(0)
    second(CORR)
    gate(1)
    total = dot(gate_out[0], half_slab(ch, 0))
    for h in range(1, HALVES):
        total = total + dot(gate_out[h], half_slab(ch, h))
    filter_grads(0)
    mix_grads(0)
    mix_grads(1)
    ghalo_out[...] = gs[:, pl.ds(0, 8), :]
    ghalo_copy.start()

    for h in range(HALVES):
        for i in others:
            gate_copies[h][i].wait_recv()
            total = total + dot(gate_in[h, i], half_slab((ch + slabs - 1 - i) % slabs, h))
    output[...] = total.astype(BF16)

    ghalo_copy.wait_recv()
    for i in range(3):
        tail = ghalo_in[i]
        ext[pl.ds(0, rows), :] = gs[i]
        ext[pl.ds(rows, 8), :] = jnp.where(s < blocks - 1, tail, jnp.zeros_like(tail))
        grad_qkv[i] = (
            sw[i, pl.ds(0, 1), :] * ext[pl.ds(0, rows), :]
            + sw[i, pl.ds(1, 1), :] * ext[pl.ds(1, rows), :]
            + sw[i, pl.ds(2, 1), :] * ext[pl.ds(2, rows), :]
        ).astype(BF16)
    filter_grads(1)

    halo_copy.wait_send()
    ghalo_copy.wait_send()
    for copies in part_copies + gate_copies:
        for copy in copies:
            copy.wait_send()
    for u in range(UNITS):
        drain(u)


def write_out(*refs):
    sem = refs[6]
    copies = [pltpu.make_async_copy(refs[i], refs[3 + i], sem.at[i]) for i in range(3)]
    for copy in copies:
        copy.start()
    for copy in copies:
        copy.wait()


def local(qkv, filt, skip_gain, short_weight, w_out, g_out):
    blocks = lax.axis_size("seq")
    slabs = lax.axis_size("ch")
    rows, width = qkv.shape[1:]
    zn = Z_CHIPS
    lines = blocks // zn
    tables = dft_tables(blocks, rows, zn)
    args = (qkv, filt, skip_gain[None, :], short_weight, w_out, g_out, *tables)
    vmem = pl.BlockSpec(memory_space=pltpu.VMEM)
    unit = (UNITS, zn, lines, OWN, rows)
    dma = pltpu.SemaphoreType.DMA
    results = pl.pallas_call(
        functools.partial(kernel, (blocks, zn, slabs, rows, width)),
        out_shape=(
            pltpu.VMEM((rows, width), BF16),
            pltpu.VMEM((3, rows, width), BF16),
            pltpu.VMEM((rows, width), F32),
        ),
        in_specs=[pl.BlockSpec(memory_space=pltpu.HBM)] * len(args),
        out_specs=(vmem, vmem, vmem),
        scratch_shapes=[
            *[pltpu.VMEM(a.shape, a.dtype) for a in args],
            dma((len(args),)),
            pltpu.VMEM(unit, BF16),
            pltpu.VMEM(unit, BF16),
            pltpu.VMEM(unit, BF16),
            pltpu.VMEM((3, 8, width), BF16),
            pltpu.VMEM((3, 8, width), F32),
            pltpu.VMEM((3, 8, width), F32),
            pltpu.VMEM((HALVES, slabs - 1, rows, width // HALVES), BF16),
            pltpu.VMEM((HALVES, slabs - 1, rows, width // HALVES), BF16),
            pltpu.VMEM((HALVES, rows, width // HALVES), BF16),
            pltpu.VMEM((HALVES, slabs - 1, rows, width // HALVES), BF16),
            pltpu.VMEM((OWN * blocks, rows), F32),
            pltpu.VMEM((rows + 8, width), F32),
            pltpu.VMEM((3 * HALVES, OWN * blocks, 2 * rows), F32),
            pltpu.VMEM((3, rows, width), F32),
            pltpu.VMEM((3, rows, width), F32),
            pltpu.VMEM((rows, width), F32),
            pltpu.VMEM((rows, width), F32),
            *[dma((UNITS,))] * 6,
            dma((4,)),
            *[dma((HALVES, slabs - 1))] * 4,
        ],
        compiler_params=pltpu.CompilerParams(
            collective_id=0, has_side_effects=True, vmem_limit_bytes=VMEM_LIMIT
        ),
    )(*(pltpu.with_memory_space_constraint(a, pltpu.HBM) for a in args))
    return pl.pallas_call(
        write_out,
        out_shape=tuple(jax.ShapeDtypeStruct(r.shape, r.dtype) for r in results),
        in_specs=[vmem] * 3,
        out_specs=[pl.BlockSpec(memory_space=pltpu.HBM)] * 3,
        scratch_shapes=[dma((3,))],
        compiler_params=pltpu.CompilerParams(vmem_limit_bytes=VMEM_LIMIT),
    )(*results)


def solution(mesh):
    in_specs = (
        P(None, "seq", "ch"),
        P("seq", "ch"),
        P("ch"),
        P(None, None, "ch"),
        P(None, "ch"),
        P("seq", "ch"),
    )
    out_specs = (P("seq", "ch"), P(None, "seq", "ch"), P("seq", "ch"))
    return jax.shard_map(local, mesh=mesh, in_specs=in_specs, out_specs=out_specs, check_vma=False)
```

```python
import functools
import math

import jax
import jax.numpy as jnp
import numpy as np
from jax import lax
from jax.experimental import pallas as pl
from jax.experimental.pallas import tpu as pltpu
from jax.sharding import PartitionSpec as P

BF16 = jnp.bfloat16
F32 = jnp.float32
MESH = pl.DeviceIdType.MESH
Z_CHIPS = 16
VMEM_LIMIT = 32 * 1024 * 1024
HALVES = 2
OWN = 2
FILT, MIXED, GRAD, CONV, CORR, GFIL = (HALVES * i for i in range(6))
UNITS = 6 * HALVES
LINE_FIRST = (FILT + 1, MIXED + 1, GRAD, GRAD + 1, CORR + 1, GFIL, GFIL + 1)


def split_const(a):
    high = a.astype(BF16)
    return high, (a - high.astype(np.float64)).astype(BF16)


def dft_tables(blocks, rows, z_chips):
    q = np.arange(blocks)
    lines = blocks // z_chips
    z, yc = q // lines, q % lines
    p = ((yc // 2) * z_chips + z) * 2 + yc % 2
    c = np.arange(blocks)[:, None] + 0.5
    outer = 2 * np.pi * p[None, :] * c / (2 * blocks)
    r = np.arange(rows)[None, :]
    turn = 2 * np.pi * r * c / (2 * blocks * rows)
    inner = 2 * np.pi * np.arange(rows)[:, None] * r / rows
    ahead = np.concatenate([np.cos(outer), -np.sin(outer)], axis=0)
    ic, is_ = np.cos(inner), np.sin(inner)
    mix = np.block([[ic, -is_], [is_, ic]])
    unmix = np.block([[ic, is_], [-is_, ic]])
    return (
        *split_const(ahead),
        *split_const(ahead.T / (blocks * rows)),
        *split_const(mix),
        *split_const(unmix),
        np.cos(turn).astype(np.float32),
        np.sin(turn).astype(np.float32),
    )


def dot(a, b):
    return jnp.dot(a, b, preferred_element_type=F32)


def halves(a):
    high = a.astype(BF16)
    return high, (a - high.astype(F32)).astype(BF16)


def kernel(shape, *refs):
    inputs, results = refs[:16], refs[16:19]
    kept, loaded = refs[19:35], refs[35]
    body(shape, inputs, kept, loaded, *results, *refs[36:])


def body(
    shape, inputs, kept, loaded,
    output, grad_qkv, grad_filter,
    send, mid, recv, halo, ghalo_out, ghalo_in, part_out, part_in, gate_out, gate_in,
    xs, ext, spec, gs, shorts, gg, glong,
    send1, recv1, send2, recv2, loc1, loc2, hsem, psend, precv, gsend, grecv, met_sem,
):
    blocks, zn, slabs, rows, width = shape
    qkv, filt, skip, sw, w_out, g_out, ah, al, bh, bl, mh, ml, uh, ul, tcos, tsin = kept
    lines = blocks // zn
    s = lax.axis_index("seq")
    ch = lax.axis_index("ch")
    core = s % 2
    z = (s // 2) % zn
    y = s // (2 * zn)
    yc = y * 2 + core

    def on_z(i):
        dz = zn // 2 + ((i + 1) // 2) * (1 - 2 * (i % 2))
        other = (z + dz) % zn
        return other, (y * zn + other) * 2 + core

    def on_line(i):
        other = (yc + 1 + i) % lines
        return other, ((other // 2) * zn + z) * 2 + other % 2

    after = (s + 1) % blocks
    before = (s + blocks - 1) % blocks

    barrier = pltpu.get_barrier_semaphore()

    def greet(a, b):
        pl.semaphore_signal(barrier, inc=1, device_id=(a, b), device_id_type=MESH)

    def on_ring(dz):
        return (y * zn + (z + dz) % zn) * 2 + core

    def greet_line(i, _):
        greet(on_line(i)[1], ch)
        return 0

    strides = [2**j for j in range(zn.bit_length() - 2)]
    near = sorted({1, zn - 1})
    for dz in near:
        greet(on_ring(dz), ch)
    lax.fori_loop(0, lines - 1, greet_line, 0)
    for i in range(1, slabs):
        greet(s, (ch + i) % slabs)
    greet(after, ch)
    greet(before, ch)

    def meet(j):
        for side, dz in enumerate((strides[j], zn - strides[j])):
            pl.semaphore_signal(
                met_sem.at[j, side], inc=1, device_id=(on_ring(dz), ch), device_id_type=MESH
            )

    def met(j):
        for side in range(2):
            pl.semaphore_wait(met_sem.at[j, side], 1)

    loads = [
        pltpu.make_async_copy(src, dst, loaded.at[i])
        for i, (src, dst) in enumerate(zip(inputs, kept))
    ]
    for i in (0, 1, 5, 4, 3, 2):
        loads[i].start()
    for copy in loads[6:]:
        copy.start()

    def slab(k):
        return w_out[pl.ds(pl.multiple_of(k * width, width), width), :]

    def rows_of(k):
        return lax.dot_general(
            g_out[...], slab(k), (((1,), (1,)), ((), ())), preferred_element_type=F32
        )

    group = width // HALVES

    def columns(h):
        return pl.ds(h * group, group)

    def pack(u, value):
        send[u] = jnp.swapaxes(value, 0, 1).astype(BF16).reshape(zn, lines, OWN, rows)

    def unpack(u):
        return jnp.swapaxes(recv[u].astype(F32).reshape(group, rows), 0, 1)

    def on_lines(u, src, dst, ssem, rsem, lsem):
        def go(i, _):
            other, device = on_line(i)
            pltpu.make_async_remote_copy(
                src_ref=src.at[u, :, other],
                dst_ref=dst.at[u, :, yc],
                send_sem=ssem.at[u],
                recv_sem=rsem.at[u],
                device_id=(device, ch),
                device_id_type=MESH,
            ).start()
            return 0

        lax.fori_loop(0, lines - 1, go, 0)
        pltpu.make_async_copy(src.at[u, :, yc], dst.at[u, :, yc], lsem.at[u]).start()

    distant = zn // 2 - 1

    def on_zs(u, src, dst, ssem, rsem, lsem, which=""):
        def go(i, _):
            other, device = on_z(i)
            pltpu.make_async_remote_copy(
                src_ref=src.at[u, other],
                dst_ref=dst.at[u, z],
                send_sem=ssem.at[u],
                recv_sem=rsem.at[u],
                device_id=(device, ch),
                device_id_type=MESH,
            ).start()
            return 0

        lax.fori_loop(distant if which == "near" else 0, distant if which == "far" else zn - 1, go, 0)
        if which != "far":
            pltpu.make_async_copy(src.at[u, z], dst.at[u, z], lsem.at[u]).start()

    def moved(u, buf, by_line, sem):
        part = buf.at[u, :, pl.ds(0, lines - 1)] if by_line else buf.at[u, pl.ds(0, zn - 1)]
        pltpu.make_async_copy(part, part, sem.at[u]).wait()

    def arrived(u, buf, by_line, rsem, lsem):
        own = buf.at[u, :, yc] if by_line else buf.at[u, z]
        pltpu.make_async_copy(own, own, lsem.at[u]).wait()
        moved(u, buf, by_line, rsem)

    def first(u):
        go = on_lines if u in LINE_FIRST else on_zs
        go(u, send, mid, send1, recv1, loc1)

    def first_part(u, which):
        on_zs(u, send, mid, send1, recv1, loc1, which)

    def second_part(u, which):
        if which == "near":
            arrived(u, mid, True, recv1, loc1)
        on_zs(u, mid, recv, send2, recv2, loc2, which)

    def second(u):
        arrived(u, mid, u in LINE_FIRST, recv1, loc1)
        go = on_zs if u in LINE_FIRST else on_lines
        go(u, mid, recv, send2, recv2, loc2)

    def finish(u):
        arrived(u, recv, u not in LINE_FIRST, recv2, loc2)

    def drain(u):
        moved(u, mid, u in LINE_FIRST, send1)
        moved(u, recv, u not in LINE_FIRST, send2)

    def to_slab(i, k, src, dst, ssem, rsem):
        return pltpu.make_async_remote_copy(
            src_ref=src,
            dst_ref=dst,
            send_sem=ssem.at[*i],
            recv_sem=rsem.at[*i],
            device_id=(s, k),
            device_id_type=MESH,
        )

    halo_copy = pltpu.make_async_remote_copy(
        src_ref=qkv.at[:, pl.ds(rows - 8, 8), :],
        dst_ref=halo,
        send_sem=hsem.at[0],
        recv_sem=hsem.at[1],
        device_id=(after, ch),
        device_id_type=MESH,
    )
    ghalo_copy = pltpu.make_async_remote_copy(
        src_ref=ghalo_out,
        dst_ref=ghalo_in,
        send_sem=hsem.at[2],
        recv_sem=hsem.at[3],
        device_id=(before, ch),
        device_id_type=MESH,
    )
    others = range(slabs - 1)
    part_copies = [
        [
            to_slab((h, i), (ch + i + 1) % slabs, part_out.at[h, i], part_in.at[h, i], psend, precv)
            for i in others
        ]
        for h in range(HALVES)
    ]
    gate_copies = [
        [
            to_slab((h, i), (ch + i + 1) % slabs, gate_out.at[h], gate_in.at[h, i], gsend, grecv)
            for i in others
        ]
        for h in range(HALVES)
    ]

    def ahead(u, k):
        xs[...] = recv[u].astype(F32).reshape(group, rows)
        x = jnp.concatenate(
            [xs[pl.ds(j, blocks, stride=OWN), :] for j in range(OWN)], axis=1
        ).astype(BF16)
        t = dot(ah[...], x) + dot(al[...], x)
        tc, ts = tcos[...], tsin[...]
        turned = []
        for j in range(OWN):
            re = t[:blocks, j * rows : (j + 1) * rows]
            im = t[blocks:, j * rows : (j + 1) * rows]
            turned.append(jnp.concatenate([re * tc + im * ts, im * tc - re * ts], axis=1))
        high, low = halves(jnp.concatenate(turned, axis=0))
        spec[k] = dot(high, mh[...]) + dot(low, mh[...]) + dot(high, ml[...])

    def back(u, re, im):
        high, low = halves(jnp.concatenate([re, im], axis=1))
        t = dot(high, uh[...]) + dot(low, uh[...]) + dot(high, ul[...])
        tc, ts = tcos[...], tsin[...]
        turned = []
        for j in range(OWN):
            re = t[j * blocks : (j + 1) * blocks, :rows]
            im = t[j * blocks : (j + 1) * blocks, rows:]
            turned.append(jnp.concatenate([re * tc - im * ts, im * tc + re * ts], axis=0))
        high, low = halves(jnp.concatenate(turned, axis=1))
        t = dot(bh[...], high) + dot(bl[...], high) + dot(bh[...], low)
        for j in range(OWN):
            xs[pl.ds(j, blocks, stride=OWN), :] = t[:, j * rows : (j + 1) * rows]
        send[u] = xs[...].astype(BF16).reshape(zn, lines, OWN, rows)

    def spectra(k, h):
        k = k + h
        return spec[k, :, :rows], spec[k, :, rows:]

    def convolve(h):
        (mre, mim), (fre, fim) = spectra(MIXED, h), spectra(FILT, h)
        back(CONV + h, mre * fre - mim * fim, mre * fim + mim * fre)
        first(CONV + h)

    def correlate(u, k, h):
        (are, aim), (gre, gim) = spectra(k, h), spectra(GRAD, h)
        back(u + h, are * gre + aim * gim, are * gim - aim * gre)
        first(u + h)

    def land(u):
        finish(u)
        ahead(u, u)

    def partial_grads(i):
        part = rows_of((ch + i + 1) % slabs).astype(BF16)
        for h in range(HALVES):
            part_out[h, i] = part[:, h * group : (h + 1) * group]
            part_copies[h][i].start()

    def shorten(i):
        head = halo[i].astype(F32)
        ext[pl.ds(0, 8), :] = jnp.where(s > 0, head, jnp.zeros_like(head))
        ext[pl.ds(8, rows), :] = qkv[i].astype(F32)
        shorts[i] = (
            sw[i, pl.ds(0, 1), :] * ext[pl.ds(8, rows), :]
            + sw[i, pl.ds(1, 1), :] * ext[pl.ds(7, rows), :]
            + sw[i, pl.ds(2, 1), :] * ext[pl.ds(6, rows), :]
        )

    steps = len(strides)
    loads[0].wait()
    pl.semaphore_wait(barrier, len(near) + lines - 1 + slabs - 1 + 2)
    if steps:
        meet(0)
    halo_copy.start()
    loads[1].wait()
    for h in reversed(range(HALVES)):
        pack(FILT + h, filt[:, columns(h)])
        if h:
            first(FILT + h)
    if steps > 2:
        met(0)
        meet(1)
    loads[5].wait()
    loads[4].wait()
    partial_grads(0)
    if steps > 1:
        met(steps - 2)
        meet(steps - 1)
    first_part(FILT, "near")
    for i in range(1, slabs - 1):
        partial_grads(i)
    second_part(FILT + 1, "near")

    halo_copy.wait_recv()
    loads[3].wait()
    loads[2].wait()
    shorten(1)
    shorten(2)
    for h in range(HALVES):
        pack(MIXED + h, shorts[1, :, columns(h)] * shorts[2, :, columns(h)])
        if h:
            first(MIXED + h)
        else:
            first_part(MIXED, "near")
    if steps:
        met(steps - 1)
    first_part(FILT, "far")
    first_part(MIXED, "far")
    second_part(FILT + 1, "far")
    gg[...] = rows_of(ch)
    shorten(0)

    def long_grads(h):
        at = columns(h)
        total = gg[:, at]
        for i in others:
            part_copies[h][i].wait_recv()
            total = total + part_in[h, i].astype(F32)
        gg[:, at] = total
        glong[:, at] = total * shorts[0, :, at]
        pack(GRAD + h, glong[:, at])
        first(GRAD + h)

    long_grads(0)
    second(MIXED + 1)
    long_grads(1)
    second(FILT)
    second(GRAD)
    second(GRAD + 1)
    second(MIXED)
    for copy in loads[6:]:
        copy.wait()
    land(FILT)
    land(FILT + 1)
    land(MIXED)
    convolve(0)
    land(MIXED + 1)
    convolve(1)
    land(GRAD)
    correlate(CORR, FILT, 0)
    correlate(GFIL, MIXED, 0)
    land(GRAD + 1)
    correlate(CORR, FILT, 1)
    second(GFIL)
    correlate(GFIL, MIXED, 1)
    second(CONV)
    second(CORR + 1)
    second(GFIL + 1)
    second(CONV + 1)

    def gate(h):
        finish(CONV + h)
        at = columns(h)
        mixed = shorts[1, :, at] * shorts[2, :, at]
        long_out = unpack(CONV + h) + skip[:, at] * mixed
        gate_out[h] = (shorts[0, :, at] * long_out).astype(BF16)
        for copy in gate_copies[h]:
            copy.start()
        gs[0, :, at] = gg[:, at] * long_out

    def mix_grads(h):
        finish(CORR + h)
        at = columns(h)
        grad_mixed = unpack(CORR + h) + skip[:, at] * glong[:, at]
        gs[1, :, at] = grad_mixed * shorts[2, :, at]
        gs[2, :, at] = grad_mixed * shorts[1, :, at]

    def filter_grads(h):
        finish(GFIL + h)
        grad_filter[:, columns(h)] = unpack(GFIL + h) * (1.0 / math.sqrt(blocks * rows))

    def half_slab(k, h):
        start = pl.multiple_of(k * width + h * group, group)
        return w_out[pl.ds(start, group), :]

    gate(0)
    second(CORR)
    gate(1)
    total = dot(gate_out[0], half_slab(ch, 0))
    for h in range(1, HALVES):
        total = total + dot(gate_out[h], half_slab(ch, h))
    filter_grads(0)
    mix_grads(0)
    mix_grads(1)
    ghalo_out[...] = gs[:, pl.ds(0, 8), :]
    ghalo_copy.start()

    for h in range(HALVES):
        for i in others:
            gate_copies[h][i].wait_recv()
            total = total + dot(gate_in[h, i], half_slab((ch + slabs - 1 - i) % slabs, h))
    output[...] = total.astype(BF16)

    ghalo_copy.wait_recv()
    for i in range(3):
        tail = ghalo_in[i]
        ext[pl.ds(0, rows), :] = gs[i]
        ext[pl.ds(rows, 8), :] = jnp.where(s < blocks - 1, tail, jnp.zeros_like(tail))
        grad_qkv[i] = (
            sw[i, pl.ds(0, 1), :] * ext[pl.ds(0, rows), :]
            + sw[i, pl.ds(1, 1), :] * ext[pl.ds(1, rows), :]
            + sw[i, pl.ds(2, 1), :] * ext[pl.ds(2, rows), :]
        ).astype(BF16)
    filter_grads(1)

    halo_copy.wait_send()
    ghalo_copy.wait_send()
    for copies in part_copies + gate_copies:
        for copy in copies:
            copy.wait_send()
    for u in range(UNITS):
        drain(u)


def write_out(*refs):
    sem = refs[6]
    copies = [pltpu.make_async_copy(refs[i], refs[3 + i], sem.at[i]) for i in range(3)]
    for copy in copies:
        copy.start()
    for copy in copies:
        copy.wait()


def local(qkv, filt, skip_gain, short_weight, w_out, g_out):
    blocks = lax.axis_size("seq")
    slabs = lax.axis_size("ch")
    rows, width = qkv.shape[1:]
    zn = Z_CHIPS
    lines = blocks // zn
    tables = dft_tables(blocks, rows, zn)
    args = (qkv, filt, skip_gain[None, :], short_weight, w_out, g_out, *tables)
    vmem = pl.BlockSpec(memory_space=pltpu.VMEM)
    unit = (UNITS, zn, lines, OWN, rows)
    dma = pltpu.SemaphoreType.DMA
    results = pl.pallas_call(
        functools.partial(kernel, (blocks, zn, slabs, rows, width)),
        out_shape=(
            pltpu.VMEM((rows, width), BF16),
            pltpu.VMEM((3, rows, width), BF16),
            pltpu.VMEM((rows, width), F32),
        ),
        in_specs=[pl.BlockSpec(memory_space=pltpu.HBM)] * len(args),
        out_specs=(vmem, vmem, vmem),
        scratch_shapes=[
            *[pltpu.VMEM(a.shape, a.dtype) for a in args],
            dma((len(args),)),
            pltpu.VMEM(unit, BF16),
            pltpu.VMEM(unit, BF16),
            pltpu.VMEM(unit, BF16),
            pltpu.VMEM((3, 8, width), BF16),
            pltpu.VMEM((3, 8, width), F32),
            pltpu.VMEM((3, 8, width), F32),
            pltpu.VMEM((HALVES, slabs - 1, rows, width // HALVES), BF16),
            pltpu.VMEM((HALVES, slabs - 1, rows, width // HALVES), BF16),
            pltpu.VMEM((HALVES, rows, width // HALVES), BF16),
            pltpu.VMEM((HALVES, slabs - 1, rows, width // HALVES), BF16),
            pltpu.VMEM((OWN * blocks, rows), F32),
            pltpu.VMEM((rows + 8, width), F32),
            pltpu.VMEM((3 * HALVES, OWN * blocks, 2 * rows), F32),
            pltpu.VMEM((3, rows, width), F32),
            pltpu.VMEM((3, rows, width), F32),
            pltpu.VMEM((rows, width), F32),
            pltpu.VMEM((rows, width), F32),
            *[dma((UNITS,))] * 6,
            dma((4,)),
            *[dma((HALVES, slabs - 1))] * 4,
            pltpu.SemaphoreType.REGULAR((3, 2)),
        ],
        compiler_params=pltpu.CompilerParams(
            collective_id=0, has_side_effects=True, vmem_limit_bytes=VMEM_LIMIT
        ),
    )(*(pltpu.with_memory_space_constraint(a, pltpu.HBM) for a in args))
    return pl.pallas_call(
        write_out,
        out_shape=tuple(jax.ShapeDtypeStruct(r.shape, r.dtype) for r in results),
        in_specs=[vmem] * 3,
        out_specs=[pl.BlockSpec(memory_space=pltpu.HBM)] * 3,
        scratch_shapes=[dma((3,))],
        compiler_params=pltpu.CompilerParams(vmem_limit_bytes=VMEM_LIMIT),
    )(*results)


def solution(mesh):
    in_specs = (
        P(None, "seq", "ch"),
        P("seq", "ch"),
        P("ch"),
        P(None, None, "ch"),
        P(None, "ch"),
        P("seq", "ch"),
    )
    out_specs = (P("seq", "ch"), P(None, "seq", "ch"), P("seq", "ch"))
    return jax.shard_map(local, mesh=mesh, in_specs=in_specs, out_specs=out_specs, check_vma=False)
```

```python
import functools
import math

import jax
import jax.numpy as jnp
import numpy as np
from jax import lax
from jax.experimental import pallas as pl
from jax.experimental.pallas import tpu as pltpu
from jax.sharding import PartitionSpec as P

BF16 = jnp.bfloat16
F32 = jnp.float32
MESH = pl.DeviceIdType.MESH
Z_CHIPS = 16
VMEM_LIMIT = 32 * 1024 * 1024
HALVES = 2
OWN = 2
FILT, MIXED, GRAD, CONV, CORR, GFIL = (HALVES * i for i in range(6))
UNITS = 6 * HALVES
LINE_FIRST = (FILT + 1, MIXED + 1, GRAD, GRAD + 1, CORR + 1, GFIL, GFIL + 1)


def split_const(a):
    high = a.astype(BF16)
    return high, (a - high.astype(np.float64)).astype(BF16)


def dft_tables(blocks, rows, z_chips):
    q = np.arange(blocks)
    lines = blocks // z_chips
    z, yc = q // lines, q % lines
    p = ((yc // 2) * z_chips + z) * 2 + yc % 2
    c = np.arange(blocks)[:, None] + 0.5
    outer = 2 * np.pi * p[None, :] * c / (2 * blocks)
    r = np.arange(rows)[None, :]
    turn = 2 * np.pi * r * c / (2 * blocks * rows)
    inner = 2 * np.pi * np.arange(rows)[:, None] * r / rows
    ahead = np.concatenate([np.cos(outer), -np.sin(outer)], axis=0)
    ic, is_ = np.cos(inner), np.sin(inner)
    mix = np.block([[ic, -is_], [is_, ic]])
    unmix = np.block([[ic, is_], [-is_, ic]])
    return (
        *split_const(ahead),
        *split_const(ahead.T / (blocks * rows)),
        *split_const(mix),
        *split_const(unmix),
        np.cos(turn).astype(np.float32),
        np.sin(turn).astype(np.float32),
    )


def dot(a, b):
    return jnp.dot(a, b, preferred_element_type=F32)


def halves(a):
    high = a.astype(BF16)
    return high, (a - high.astype(F32)).astype(BF16)


def kernel(shape, *refs):
    inputs, results = refs[:16], refs[16:19]
    kept, loaded = refs[19:35], refs[35]
    body(shape, inputs, kept, loaded, *results, *refs[36:])


def body(
    shape, inputs, kept, loaded,
    output, grad_qkv, grad_filter,
    send, mid, recv, halo, ghalo_out, ghalo_in, part_out, part_in, gate_out, gate_in,
    xs, ext, spec, gs, shorts, gg, glong,
    send1, recv1, send2, recv2, loc1, loc2, hsem, psend, precv, gsend, grecv,
):
    blocks, zn, slabs, rows, width = shape
    qkv, filt, skip, sw, w_out, g_out, ah, al, bh, bl, mh, ml, uh, ul, tcos, tsin = kept
    lines = blocks // zn
    s = lax.axis_index("seq")
    ch = lax.axis_index("ch")
    core = s % 2
    z = (s // 2) % zn
    y = s // (2 * zn)
    yc = y * 2 + core

    def on_z(i):
        dz = zn // 2 + ((i + 1) // 2) * (1 - 2 * (i % 2))
        other = (z + dz) % zn
        return other, (y * zn + other) * 2 + core

    def on_line(i):
        other = (yc + 1 + i) % lines
        return other, ((other // 2) * zn + z) * 2 + other % 2

    after = (s + 1) % blocks
    before = (s + blocks - 1) % blocks

    barrier = pltpu.get_barrier_semaphore()

    def greet(a, b):
        pl.semaphore_signal(barrier, inc=1, device_id=(a, b), device_id_type=MESH)

    def greet_z(i, _):
        greet(on_z(i)[1], ch)
        return 0

    def greet_line(i, _):
        greet(on_line(i)[1], ch)
        return 0

    lax.fori_loop(0, zn - 1, greet_z, 0)
    lax.fori_loop(0, lines - 1, greet_line, 0)
    for i in range(1, slabs):
        greet(s, (ch + i) % slabs)
    greet(after, ch)
    greet(before, ch)

    loads = [
        pltpu.make_async_copy(src, dst, loaded.at[i])
        for i, (src, dst) in enumerate(zip(inputs, kept))
    ]
    for i in (5, 4, 1, 0, 3, 2):
        loads[i].start()
    for copy in loads[6:]:
        copy.start()

    def slab(k):
        return w_out[pl.ds(pl.multiple_of(k * width, width), width), :]

    def rows_of(k):
        return lax.dot_general(
            g_out[...], slab(k), (((1,), (1,)), ((), ())), preferred_element_type=F32
        )

    group = width // HALVES

    def columns(h):
        return pl.ds(h * group, group)

    def pack(u, value):
        send[u] = jnp.swapaxes(value, 0, 1).astype(BF16).reshape(zn, lines, OWN, rows)

    def unpack(u):
        return jnp.swapaxes(recv[u].astype(F32).reshape(group, rows), 0, 1)

    def on_lines(u, src, dst, ssem, rsem, lsem):
        def go(i, _):
            other, device = on_line(i)
            pltpu.make_async_remote_copy(
                src_ref=src.at[u, :, other],
                dst_ref=dst.at[u, :, yc],
                send_sem=ssem.at[u],
                recv_sem=rsem.at[u],
                device_id=(device, ch),
                device_id_type=MESH,
            ).start()
            return 0

        lax.fori_loop(0, lines - 1, go, 0)
        pltpu.make_async_copy(src.at[u, :, yc], dst.at[u, :, yc], lsem.at[u]).start()

    def on_zs(u, src, dst, ssem, rsem, lsem):
        def go(i, _):
            other, device = on_z(i)
            pltpu.make_async_remote_copy(
                src_ref=src.at[u, other],
                dst_ref=dst.at[u, z],
                send_sem=ssem.at[u],
                recv_sem=rsem.at[u],
                device_id=(device, ch),
                device_id_type=MESH,
            ).start()
            return 0

        lax.fori_loop(0, zn - 1, go, 0)
        pltpu.make_async_copy(src.at[u, z], dst.at[u, z], lsem.at[u]).start()

    def moved(u, buf, by_line, sem):
        part = buf.at[u, :, pl.ds(0, lines - 1)] if by_line else buf.at[u, pl.ds(0, zn - 1)]
        pltpu.make_async_copy(part, part, sem.at[u]).wait()

    def arrived(u, buf, by_line, rsem, lsem):
        own = buf.at[u, :, yc] if by_line else buf.at[u, z]
        pltpu.make_async_copy(own, own, lsem.at[u]).wait()
        moved(u, buf, by_line, rsem)

    def first(u):
        go = on_lines if u in LINE_FIRST else on_zs
        go(u, send, mid, send1, recv1, loc1)

    def second(u):
        arrived(u, mid, u in LINE_FIRST, recv1, loc1)
        go = on_zs if u in LINE_FIRST else on_lines
        go(u, mid, recv, send2, recv2, loc2)

    def finish(u):
        arrived(u, recv, u not in LINE_FIRST, recv2, loc2)

    def drain(u):
        moved(u, mid, u in LINE_FIRST, send1)
        moved(u, recv, u not in LINE_FIRST, send2)

    def to_slab(i, k, src, dst, ssem, rsem):
        return pltpu.make_async_remote_copy(
            src_ref=src,
            dst_ref=dst,
            send_sem=ssem.at[*i],
            recv_sem=rsem.at[*i],
            device_id=(s, k),
            device_id_type=MESH,
        )

    halo_copy = pltpu.make_async_remote_copy(
        src_ref=qkv.at[:, pl.ds(rows - 8, 8), :],
        dst_ref=halo,
        send_sem=hsem.at[0],
        recv_sem=hsem.at[1],
        device_id=(after, ch),
        device_id_type=MESH,
    )
    ghalo_copy = pltpu.make_async_remote_copy(
        src_ref=ghalo_out,
        dst_ref=ghalo_in,
        send_sem=hsem.at[2],
        recv_sem=hsem.at[3],
        device_id=(before, ch),
        device_id_type=MESH,
    )
    others = range(slabs - 1)
    part_copies = [
        [
            to_slab((h, i), (ch + i + 1) % slabs, part_out.at[h, i], part_in.at[h, i], psend, precv)
            for i in others
        ]
        for h in range(HALVES)
    ]
    gate_copies = [
        [
            to_slab((h, i), (ch + i + 1) % slabs, gate_out.at[h], gate_in.at[h, i], gsend, grecv)
            for i in others
        ]
        for h in range(HALVES)
    ]

    def ahead(u, k):
        xs[...] = recv[u].astype(F32).reshape(group, rows)
        x = jnp.concatenate(
            [xs[pl.ds(j, blocks, stride=OWN), :] for j in range(OWN)], axis=1
        ).astype(BF16)
        t = dot(ah[...], x) + dot(al[...], x)
        tc, ts = tcos[...], tsin[...]
        turned = []
        for j in range(OWN):
            re = t[:blocks, j * rows : (j + 1) * rows]
            im = t[blocks:, j * rows : (j + 1) * rows]
            turned.append(jnp.concatenate([re * tc + im * ts, im * tc - re * ts], axis=1))
        high, low = halves(jnp.concatenate(turned, axis=0))
        spec[k] = dot(high, mh[...]) + dot(low, mh[...]) + dot(high, ml[...])

    def back(u, re, im):
        high, low = halves(jnp.concatenate([re, im], axis=1))
        t = dot(high, uh[...]) + dot(low, uh[...]) + dot(high, ul[...])
        tc, ts = tcos[...], tsin[...]
        turned = []
        for j in range(OWN):
            re = t[j * blocks : (j + 1) * blocks, :rows]
            im = t[j * blocks : (j + 1) * blocks, rows:]
            turned.append(jnp.concatenate([re * tc - im * ts, im * tc + re * ts], axis=0))
        high, low = halves(jnp.concatenate(turned, axis=1))
        t = dot(bh[...], high) + dot(bl[...], high) + dot(bh[...], low)
        for j in range(OWN):
            xs[pl.ds(j, blocks, stride=OWN), :] = t[:, j * rows : (j + 1) * rows]
        send[u] = xs[...].astype(BF16).reshape(zn, lines, OWN, rows)

    def spectra(k, h):
        k = k + h
        return spec[k, :, :rows], spec[k, :, rows:]

    def convolve(h):
        (mre, mim), (fre, fim) = spectra(MIXED, h), spectra(FILT, h)
        back(CONV + h, mre * fre - mim * fim, mre * fim + mim * fre)
        first(CONV + h)

    def correlate(u, k, h):
        (are, aim), (gre, gim) = spectra(k, h), spectra(GRAD, h)
        back(u + h, are * gre + aim * gim, are * gim - aim * gre)
        first(u + h)

    def land(u):
        finish(u)
        ahead(u, u)

    loads[5].wait()
    loads[4].wait()
    for i in others:
        part = rows_of((ch + i + 1) % slabs).astype(BF16)
        for h in range(HALVES):
            part_out[h, i] = part[:, h * group : (h + 1) * group]
    loads[1].wait()
    for h in range(HALVES):
        pack(FILT + h, filt[:, columns(h)])
    gg[...] = rows_of(ch)
    for i in (0, 3, 2):
        loads[i].wait()
    pl.semaphore_wait(barrier, zn - 1 + lines - 1 + slabs - 1 + 2)

    for copy in part_copies[0]:
        copy.start()
    halo_copy.start()
    first(FILT)
    for copies in part_copies[1:]:
        for copy in copies:
            copy.start()
    first(FILT + 1)

    def shorten(i):
        head = halo[i].astype(F32)
        ext[pl.ds(0, 8), :] = jnp.where(s > 0, head, jnp.zeros_like(head))
        ext[pl.ds(8, rows), :] = qkv[i].astype(F32)
        shorts[i] = (
            sw[i, pl.ds(0, 1), :] * ext[pl.ds(8, rows), :]
            + sw[i, pl.ds(1, 1), :] * ext[pl.ds(7, rows), :]
            + sw[i, pl.ds(2, 1), :] * ext[pl.ds(6, rows), :]
        )

    halo_copy.wait_recv()
    shorten(1)
    shorten(2)
    for h in range(HALVES):
        pack(MIXED + h, shorts[1, :, columns(h)] * shorts[2, :, columns(h)])
        first(MIXED + h)
    second(FILT + 1)
    shorten(0)

    def long_grads(h):
        at = columns(h)
        total = gg[:, at]
        for i in others:
            part_copies[h][i].wait_recv()
            total = total + part_in[h, i].astype(F32)
        gg[:, at] = total
        glong[:, at] = total * shorts[0, :, at]
        pack(GRAD + h, glong[:, at])
        first(GRAD + h)

    long_grads(0)
    second(MIXED + 1)
    long_grads(1)
    second(FILT)
    second(GRAD)
    second(GRAD + 1)
    second(MIXED)
    for copy in loads[6:]:
        copy.wait()
    land(FILT)
    land(FILT + 1)
    land(MIXED)
    convolve(0)
    land(MIXED + 1)
    convolve(1)
    land(GRAD)
    correlate(CORR, FILT, 0)
    correlate(GFIL, MIXED, 0)
    land(GRAD + 1)
    correlate(CORR, FILT, 1)
    second(GFIL)
    correlate(GFIL, MIXED, 1)
    second(CONV)
    second(CORR + 1)
    second(GFIL + 1)
    second(CONV + 1)

    def gate(h):
        finish(CONV + h)
        at = columns(h)
        mixed = shorts[1, :, at] * shorts[2, :, at]
        long_out = unpack(CONV + h) + skip[:, at] * mixed
        gate_out[h] = (shorts[0, :, at] * long_out).astype(BF16)
        for copy in gate_copies[h]:
            copy.start()
        gs[0, :, at] = gg[:, at] * long_out

    def mix_grads(h):
        finish(CORR + h)
        at = columns(h)
        grad_mixed = unpack(CORR + h) + skip[:, at] * glong[:, at]
        gs[1, :, at] = grad_mixed * shorts[2, :, at]
        gs[2, :, at] = grad_mixed * shorts[1, :, at]

    def filter_grads(h):
        finish(GFIL + h)
        grad_filter[:, columns(h)] = unpack(GFIL + h) * (1.0 / math.sqrt(blocks * rows))

    def half_slab(k, h):
        start = pl.multiple_of(k * width + h * group, group)
        return w_out[pl.ds(start, group), :]

    gate(0)
    second(CORR)
    gate(1)
    total = dot(gate_out[0], half_slab(ch, 0))
    for h in range(1, HALVES):
        total = total + dot(gate_out[h], half_slab(ch, h))
    filter_grads(0)
    mix_grads(0)
    mix_grads(1)
    ghalo_out[...] = gs[:, pl.ds(0, 8), :]
    ghalo_copy.start()

    for h in range(HALVES):
        for i in others:
            gate_copies[h][i].wait_recv()
            total = total + dot(gate_in[h, i], half_slab((ch + slabs - 1 - i) % slabs, h))
    output[...] = total.astype(BF16)

    ghalo_copy.wait_recv()
    for i in range(3):
        tail = ghalo_in[i]
        ext[pl.ds(0, rows), :] = gs[i]
        ext[pl.ds(rows, 8), :] = jnp.where(s < blocks - 1, tail, jnp.zeros_like(tail))
        grad_qkv[i] = (
            sw[i, pl.ds(0, 1), :] * ext[pl.ds(0, rows), :]
            + sw[i, pl.ds(1, 1), :] * ext[pl.ds(1, rows), :]
            + sw[i, pl.ds(2, 1), :] * ext[pl.ds(2, rows), :]
        ).astype(BF16)
    filter_grads(1)

    halo_copy.wait_send()
    ghalo_copy.wait_send()
    for copies in part_copies + gate_copies:
        for copy in copies:
            copy.wait_send()
    for u in range(UNITS):
        drain(u)


def write_out(*refs):
    sem = refs[6]
    copies = [pltpu.make_async_copy(refs[i], refs[3 + i], sem.at[i]) for i in range(3)]
    for copy in copies:
        copy.start()
    for copy in copies:
        copy.wait()


def local(qkv, filt, skip_gain, short_weight, w_out, g_out):
    blocks = lax.axis_size("seq")
    slabs = lax.axis_size("ch")
    rows, width = qkv.shape[1:]
    zn = Z_CHIPS
    lines = blocks // zn
    tables = dft_tables(blocks, rows, zn)
    args = (qkv, filt, skip_gain[None, :], short_weight, w_out, g_out, *tables)
    vmem = pl.BlockSpec(memory_space=pltpu.VMEM)
    unit = (UNITS, zn, lines, OWN, rows)
    dma = pltpu.SemaphoreType.DMA
    results = pl.pallas_call(
        functools.partial(kernel, (blocks, zn, slabs, rows, width)),
        out_shape=(
            pltpu.VMEM((rows, width), BF16),
            pltpu.VMEM((3, rows, width), BF16),
            pltpu.VMEM((rows, width), F32),
        ),
        in_specs=[pl.BlockSpec(memory_space=pltpu.HBM)] * len(args),
        out_specs=(vmem, vmem, vmem),
        scratch_shapes=[
            *[pltpu.VMEM(a.shape, a.dtype) for a in args],
            dma((len(args),)),
            pltpu.VMEM(unit, BF16),
            pltpu.VMEM(unit, BF16),
            pltpu.VMEM(unit, BF16),
            pltpu.VMEM((3, 8, width), BF16),
            pltpu.VMEM((3, 8, width), F32),
            pltpu.VMEM((3, 8, width), F32),
            pltpu.VMEM((HALVES, slabs - 1, rows, width // HALVES), BF16),
            pltpu.VMEM((HALVES, slabs - 1, rows, width // HALVES), BF16),
            pltpu.VMEM((HALVES, rows, width // HALVES), BF16),
            pltpu.VMEM((HALVES, slabs - 1, rows, width // HALVES), BF16),
            pltpu.VMEM((OWN * blocks, rows), F32),
            pltpu.VMEM((rows + 8, width), F32),
            pltpu.VMEM((3 * HALVES, OWN * blocks, 2 * rows), F32),
            pltpu.VMEM((3, rows, width), F32),
            pltpu.VMEM((3, rows, width), F32),
            pltpu.VMEM((rows, width), F32),
            pltpu.VMEM((rows, width), F32),
            *[dma((UNITS,))] * 6,
            dma((4,)),
            *[dma((HALVES, slabs - 1))] * 4,
        ],
        compiler_params=pltpu.CompilerParams(
            collective_id=0, has_side_effects=True, vmem_limit_bytes=VMEM_LIMIT
        ),
    )(*(pltpu.with_memory_space_constraint(a, pltpu.HBM) for a in args))
    return pl.pallas_call(
        write_out,
        out_shape=tuple(jax.ShapeDtypeStruct(r.shape, r.dtype) for r in results),
        in_specs=[vmem] * 3,
        out_specs=[pl.BlockSpec(memory_space=pltpu.HBM)] * 3,
        scratch_shapes=[dma((3,))],
        compiler_params=pltpu.CompilerParams(vmem_limit_bytes=VMEM_LIMIT),
    )(*results)


def solution(mesh):
    in_specs = (
        P(None, "seq", "ch"),
        P("seq", "ch"),
        P("ch"),
        P(None, None, "ch"),
        P(None, "ch"),
        P("seq", "ch"),
    )
    out_specs = (P("seq", "ch"), P(None, "seq", "ch"), P("seq", "ch"))
    return jax.shard_map(local, mesh=mesh, in_specs=in_specs, out_specs=out_specs, check_vma=False)
```
